128 devices in a mesh: expert: 32 (over z, y, x_hi), dp: 4 (over x_lo, core).
Axes of the slice: x: 4 (x_hi: 2, x_lo: 2; x = x_hi * 2 + x_lo), y: 4, z: 4, core: 2. Of those that a mesh axis runs over, the one named last changes fastest.
Arguments:
- tokens: bfloat16 [16384, 3584], P(('expert', 'dp')), may hold values from -6 to 6
- out_grad: bfloat16 [16384, 3584], P(('expert', 'dp')), may hold values from -2 to 2
- expert_ids: int32 [16384, 8], P(('expert', 'dp')), may hold values from 0 to 255, as said below
- route_weights: bfloat16 [16384, 8], P(('expert', 'dp')), may hold values from 0.099609375 to 1
- w_gate: bfloat16 [32, 3584, 1024], P('expert', None, 'dp'), may hold values from -0.09375 to 0.09375
- w_up: bfloat16 [32, 3584, 1024], P('expert', None, 'dp'), may hold values from -0.09375 to 0.09375
- w_down: bfloat16 [32, 1024, 3584], P('expert', 'dp'), may hold values from -0.1875 to 0.1875
Outputs:
- grad_tokens: bfloat16 [16384, 3584], P(('expert', 'dp'))
- grad_route: bfloat16 [16384, 8], P(('expert', 'dp'))
- grad_gate: bfloat16 [32, 3584, 1024], P('expert', None, 'dp')
- grad_upproj: bfloat16 [32, 3584, 1024], P('expert', None, 'dp')
- grad_down: bfloat16 [32, 1024, 3584], P('expert', 'dp')
The draws below stay inside these ranges and needn't reach their ends.
Inputs may be any that keep to these rules, and one draw needn't show every extreme that they name: `expert_ids`: each token's 8 ids are distinct. Ids below 32 are the window's experts. Within the 128 tokens of one device no id below 32 appears more than 5 times.
All inputs are finite; a program needn't handle non-finite values.
Results may differ from the reference program's by a relative error of at most 0.015.
Values may be sent and summed in bfloat16 or wider, within the bound.
A program may use at most 128 MiB of HBM per device.

```python
import math
import jax
import jax.numpy as jnp
from jax import lax

D = 3584
FF = 1024
TOPK = 8
TOK_DEV = 128
EXPERTS = 32
ALL_EXPERTS = 256
CAP = 5
GROUPS = 4
FF_DEV = 256
TOKENS = 16384


def draw_expert_ids(key, part):
    block_count = TOKENS // TOK_DEV
    route_slots = TOK_DEV * TOPK
    key_hot, key_window, key_shuffle, key_routes = jax.random.split(jax.random.fold_in(key, 11), 4)
    hot_experts = jax.random.permutation(key_hot, EXPERTS)[:2]
    is_hot = jnp.any(jnp.arange(EXPERTS)[:, None] == hot_experts[None, :], axis=1)
    upper_count = 3 * CAP // 5 + 1
    window_counts = jax.random.randint(key_window, (block_count, EXPERTS), 1, upper_count + 1)
    window_counts = jnp.minimum(window_counts, upper_count)
    window_counts = jnp.where(is_hot[None, :], CAP, window_counts)
    remainder = route_slots - jnp.sum(window_counts, axis=1)
    others = ALL_EXPERTS - EXPERTS
    other_index = jnp.arange(others)
    other_counts = remainder[:, None] // others + (other_index[None, :] < remainder[:, None] % others).astype(jnp.int32)
    counts = jnp.concatenate([window_counts, other_counts], axis=1)
    cumulative = jnp.cumsum(counts, axis=1)
    position = jnp.arange(route_slots)
    route_ids = jax.vmap(lambda bounds: jnp.searchsorted(bounds, position, side='right'))(cumulative)
    route_ids = route_ids.reshape(block_count, TOPK, TOK_DEV).transpose(0, 2, 1)
    block_keys = jax.random.split(key_shuffle, block_count)
    shuffle = jax.vmap(lambda one_key: jax.random.permutation(one_key, TOK_DEV))(block_keys)
    route_ids = jnp.take_along_axis(route_ids, shuffle[:, :, None], axis=1)
    scores = jax.random.randint(key_routes, (block_count, TOK_DEV, TOPK), 0, 1000) * TOPK + jnp.arange(TOPK)[None, None, :]
    route_order = jnp.argsort(scores, axis=2)
    route_ids = jnp.take_along_axis(route_ids, route_order, axis=2)
    return route_ids.reshape(TOKENS, TOPK).astype(jnp.int32)


def level_of(stream_key, shape, pieces, least, largest):
    factor_of = 1.0
    for dim, parts in pieces:
        draws = jax.random.uniform(jax.random.fold_in(jax.random.fold_in(stream_key, 6), dim), (parts,), jnp.float32, least / len(pieces), largest / len(pieces))
        factor_of = factor_of * jnp.repeat(jnp.exp(draws), shape[dim] // parts).reshape((-1,) + (1,) * (len(shape) - 1 - dim))
    return factor_of


def centred(own_key, shape, width, reach, cuts=(), held_as=jnp.bfloat16):
    entries = jax.random.normal(own_key, shape, jnp.float32) * width
    if len(cuts) > 0:
        entries = level_of(own_key, shape, cuts, -0.22, 0.18) * entries
    return jnp.clip(entries, min=-reach, max=reach).astype(held_as)


def setup_inputs(seed: int = 0) -> dict:
    key_of = jax.random.split(jax.random.key(seed), 8)
    return {
        "tokens": centred(key_of[0], (TOKENS, D), 1.0, 6.0, ((0, 128),)),
        "out_grad": centred(key_of[1], (TOKENS, D), 0.3, 2.0, ((0, 128),)),
        "expert_ids": draw_expert_ids(jax.random.fold_in(key_of[7], 71), 0),
        "route_weights": jnp.clip(jnp.exp(math.log(1.0) - 2.306499 * jax.random.uniform(key_of[3], (TOKENS, TOPK), jnp.float32) ** level_of(key_of[3], (TOKENS, TOPK), ((0, 128),), -0.2, 0.2)), 0.099609375, 1.0).astype(jnp.bfloat16),
        "w_gate": centred(key_of[4], (EXPERTS, D, FF), D ** -0.5, 0.09375, ((0, 32), (2, 4))),
        "w_up": centred(key_of[5], (EXPERTS, D, FF), D ** -0.5, 0.09375, ((0, 32), (2, 4))),
        "w_down": centred(key_of[6], (EXPERTS, FF, D), FF ** -0.5, 0.1875, ((0, 32), (1, 4))),
    }


def rounded_back(values):
    return lax.optimization_barrier(values.astype(jnp.bfloat16)).astype(jnp.float32)


def reference(tokens, out_grad, expert_ids, route_weights, w_gate, w_up, w_down):
    block_count = TOKENS // TOK_DEV
    route_slots = TOK_DEV * TOPK
    flat_ids = expert_ids.reshape(block_count, route_slots)
    onehot = (flat_ids[:, :, None] == jnp.arange(EXPERTS, dtype=jnp.int32)[None, None, :]).astype(jnp.int32)
    ranking = jnp.sum((jnp.cumsum(onehot, axis=1) - 1) * onehot, axis=2)
    target = jnp.where(flat_ids < EXPERTS, flat_ids * CAP + ranking, EXPERTS * CAP).astype(jnp.int32)
    local_index = jnp.arange(route_slots, dtype=jnp.int32)

    def fill_slots(dest):
        return jnp.full((EXPERTS * CAP,), -1, jnp.int32).at[dest].set(local_index, mode="drop")

    slot_table = jax.vmap(fill_slots)(target)
    offsets = (jnp.arange(block_count, dtype=jnp.int32) * route_slots)[:, None]
    global_table = jnp.where(slot_table >= 0, slot_table + offsets, -1)
    per_expert = global_table.reshape(block_count, EXPERTS, CAP).transpose(1, 0, 2).reshape(EXPERTS, block_count * CAP)
    flat_weights = route_weights.reshape(-1).astype(jnp.float32)

    def one_expert(carry, inputs):
        grad_sum, route_sum = carry
        slot_index, gate_w, up_w, down_w = inputs
        occupied = slot_index >= 0
        clamped = jnp.where(occupied, slot_index, 0)
        owner_token = clamped // TOPK
        x_rows = tokens[owner_token]
        dy_rows = out_grad[owner_token]
        weight = jnp.where(occupied, flat_weights[clamped], 0.0)[:, None]
        gate_value = jnp.dot(x_rows, gate_w, preferred_element_type=jnp.float32)
        up_value = jnp.dot(x_rows, up_w, preferred_element_type=jnp.float32)
        sigmoid_gate = jax.nn.sigmoid(gate_value)
        hidden = (gate_value * sigmoid_gate * up_value).astype(jnp.bfloat16)
        back_proj = lax.dot_general(dy_rows, down_w, (((1,), (1,)), ((), ())), preferred_element_type=jnp.float32)
        row_count = x_rows.shape[0]
        hidden_f = hidden.astype(jnp.float32)
        group_route = jnp.sum((hidden_f * back_proj).reshape(row_count, GROUPS, FF_DEV), axis=2)
        route_value = jnp.sum(rounded_back(group_route), axis=1).astype(jnp.bfloat16)
        scaled = weight * back_proj
        d_gate = (scaled * up_value * sigmoid_gate * (1.0 + gate_value * (1.0 - sigmoid_gate))).astype(jnp.bfloat16)
        d_up = (scaled * gate_value * sigmoid_gate).astype(jnp.bfloat16)
        weighted = (weight * hidden_f).astype(jnp.bfloat16)
        contract_rows = (((0,), (0,)), ((), ()))
        grad_g = lax.dot_general(x_rows, d_gate, contract_rows, preferred_element_type=jnp.float32).astype(jnp.bfloat16)
        grad_u = lax.dot_general(x_rows, d_up, contract_rows, preferred_element_type=jnp.float32).astype(jnp.bfloat16)
        grad_d = lax.dot_general(weighted, dy_rows, contract_rows, preferred_element_type=jnp.float32).astype(jnp.bfloat16)
        gate_groups = gate_w.astype(jnp.float32).reshape(D, GROUPS, FF_DEV)
        up_groups = up_w.astype(jnp.float32).reshape(D, GROUPS, FF_DEV)
        dg_groups = d_gate.astype(jnp.float32).reshape(row_count, GROUPS, FF_DEV)
        du_groups = d_up.astype(jnp.float32).reshape(row_count, GROUPS, FF_DEV)
        group_part = jnp.einsum("rqf,dqf->rqd", dg_groups, gate_groups) + jnp.einsum("rqf,dqf->rqd", du_groups, up_groups)
        contrib = jnp.sum(rounded_back(group_part), axis=1)
        contrib_f = rounded_back(contrib)
        token_target = jnp.where(occupied, owner_token, TOKENS)
        grad_sum = grad_sum.at[token_target].add(contrib_f, mode="drop")
        route_target = jnp.where(occupied, clamped, TOKENS * TOPK)
        route_sum = route_sum.at[route_target].set(route_value.astype(jnp.float32), mode="drop")
        return (grad_sum, route_sum), (grad_g, grad_u, grad_d)

    start = (jnp.zeros((TOKENS, D), jnp.float32), jnp.zeros((TOKENS * TOPK,), jnp.float32))
    (grad_sum, route_sum), (grad_gate, grad_upproj, grad_down) = lax.scan(one_expert, start, (per_expert, w_gate, w_up, w_down))
    return (grad_sum.astype(jnp.bfloat16), route_sum.reshape(TOKENS, TOPK).astype(jnp.bfloat16), grad_gate, grad_upproj, grad_down)
```

```python
import jax
import jax.numpy as jnp
from jax import lax
from jax.experimental import pallas as pl
from jax.experimental.pallas import tpu as pltpu
from jax.sharding import PartitionSpec as P

NZ, NY, NX = 4, 4, 2
EXP = NZ * NY * NX
CAP = 5
STEP = 4
CHUNKS = EXP // STEP
LANES = 128
FEAT = 3584
HID = 256
COLS = FEAT // LANES
FROWS = 288
RROWS = 144
SRC = 4 * STEP
ROWS = SRC * CAP
ALL = ROWS * CHUNKS
TOK = 128
MESH = pl.DeviceIdType.MESH
F32, BF16 = jnp.float32, jnp.bfloat16


def shifted(e, k, sign):
    z, y, x = e // (NY * NX), (e // NX) % NY, e % NX
    kz, ky, kx = k // (NY * NX), (k // NX) % NY, k % NX
    z = (z + NZ + sign * kz) % NZ
    y = (y + NY + sign * ky) % NY
    x = (x + NX + sign * kx) % NX
    return (z * NY + y) * NX + x


def body(
    ids_ref, rw_ref, tok_ref, dy_ref, wg_hbm, wu_hbm, wd_hbm,
    gt_ref, gr_ref, gg_hbm, gu_hbm, gd_hbm,
    wg, wu, wd, flat, send, recv, rows, dgu, wtd, retf, own, pst, prt, rsend, ret, slots, got, sg, su, sd,
    send_sem, recv_sem, fws_sem, fwr_sem, pas_sem, par_sem, rs_sem, ret_sem, win_sem, out_sem,
):
    e = lax.axis_index("expert")
    d = lax.axis_index("dp")
    xl, c = d // 2, d % 2
    partner = {"expert": e, "dp": xl * 2 + 1 - c}

    loads = [
        pltpu.make_async_copy(h, v, win_sem.at[i])
        for i, (h, v) in enumerate(((wg_hbm, wg), (wu_hbm, wu), (wd_hbm, wd)))
    ]
    for copy in loads:
        copy.start()

    kk = lax.broadcasted_iota(jnp.int32, (EXP, TOK), 0)
    z, y, x = e // (NY * NX), (e // NX) % NY, e % NX
    tz = (z + (kk >> 3)) & 3
    ty = (y + ((kk >> 1) & 3)) & 3
    tx = (x + (kk & 1)) & 1
    target = tz * (NY * NX) + ty * NX + tx
    chosen = jnp.zeros((EXP, TOK), F32)
    weight = jnp.zeros((EXP, TOK), F32)
    for q in range(8):
        same = ids_ref[q : q + 1, :] == target
        chosen = chosen + jnp.where(same, 1.0, 0.0)
        weight = weight + jnp.where(same, rw_ref[q : q + 1, :], 0.0)
    before = lax.broadcasted_iota(jnp.int32, (TOK, TOK), 0) < lax.broadcasted_iota(
        jnp.int32, (TOK, TOK), 1
    )
    rank = jnp.dot(
        chosen.astype(BF16), jnp.where(before, 1.0, 0.0).astype(BF16), preferred_element_type=F32
    )
    for j in range(CAP):
        hot = jnp.where(jnp.abs(rank - j) < 0.5, chosen, 0.0)
        slots[j * EXP : (j + 1) * EXP, :] = hot.astype(BF16)
        one = jnp.sum(hot * weight, axis=1, keepdims=True)
        flat[pl.ds(2 * CAP * COLS + j, EXP, stride=FROWS), :] = jnp.broadcast_to(one, (EXP, LANES))
    for j in range(2 * CAP * COLS + CAP, FROWS):
        flat[pl.ds(j, EXP, stride=FROWS), :] = jnp.zeros((EXP, LANES), F32)
    for j in range(CAP * COLS + 1, RROWS):
        retf[pl.ds(j, SRC, stride=RROWS), :] = jnp.zeros((SRC, LANES), F32)

    def gather(m, carry):
        for a, ref in enumerate((tok_ref, dy_ref)):
            picked = jnp.dot(
                slots[...], ref[:, pl.ds(pl.multiple_of(m * 256, 256), 256)], preferred_element_type=F32
            )
            for h in range(2):
                for j in range(CAP):
                    at = j * 2 * COLS + a * COLS + m * 2 + h
                    flat[pl.ds(at, EXP, stride=FROWS), :] = picked[
                        j * EXP : (j + 1) * EXP, h * LANES : (h + 1) * LANES
                    ]
        return carry

    lax.fori_loop(0, FEAT // 256, gather, 0)

    def remote(k, xd):
        g, kq = k // STEP, k % STEP
        return pltpu.make_async_remote_copy(
            src_ref=send.at[k],
            dst_ref=recv.at[g, c * (2 * STEP) + kq * 2 + xl],
            send_sem=send_sem.at[k * 2 + xd],
            recv_sem=recv_sem.at[g],
            device_id={"expert": shifted(e, k, 1), "dp": xd * 2 + c},
            device_id_type=MESH,
        )

    send[0] = flat[0:FROWS, :].astype(BF16)
    remote(0, 1 - xl).start()
    pltpu.make_async_copy(send.at[0], recv.at[0, c * (2 * STEP) + xl], recv_sem.at[0]).start()

    def issue(k, carry):
        send[k] = flat[pl.ds(pl.multiple_of(k * FROWS, 8), FROWS), :].astype(BF16)
        remote(k, 0).start()
        remote(k, 1).start()
        return carry

    lax.fori_loop(1, EXP, issue, 0)
    for copy in loads:
        copy.wait()

    def half(g, core):
        return recv.at[g, pl.ds(core * (2 * STEP), 2 * STEP)]

    def forward(g):
        return pltpu.make_async_remote_copy(
            src_ref=half(g, c), dst_ref=half(g, c), send_sem=fws_sem.at[g], recv_sem=fwr_sem.at[g],
            device_id=partner, device_id_type=MESH,
        )

    def take(g):
        pltpu.make_async_copy(half(g, c), half(g, c), recv_sem.at[g]).wait()
        forward(g).start()

    def part(g):
        return pltpu.make_async_remote_copy(
            src_ref=pst.at[g], dst_ref=prt.at[g], send_sem=pas_sem.at[g], recv_sem=par_sem.at[g],
            device_id=partner, device_id_type=MESH,
        )

    def back(g, i, xs):
        kq = i // 2
        return pltpu.make_async_remote_copy(
            src_ref=rsend.at[g, pl.ds(pl.multiple_of((kq * 2 + xs) * RROWS, 16), RROWS)],
            dst_ref=ret.at[g, xl * STEP + kq],
            send_sem=rs_sem.at[g * (2 * STEP) + i],
            recv_sem=ret_sem.at[g],
            device_id={"expert": shifted(e, g * STEP + kq, -1), "dp": xs * 2 + c},
            device_id_type=MESH,
        )

    def compute(g):
        def widen(s, carry):
            flat[pl.ds(pl.multiple_of(s * FROWS, 8), FROWS), :] = recv[g, s].astype(F32)
            return carry

        lax.fori_loop(0, SRC, widen, 0)
        base = pl.multiple_of(g * ROWS, 16)

        def order(q, carry):
            for h in range(4):
                col = q * 4 + h
                for j in range(CAP):
                    piece = flat[pl.ds(j * 2 * COLS + col, SRC, stride=FROWS), :]
                    rows[
                        pl.ds(pl.multiple_of(base + j * SRC, 16), SRC),
                        pl.ds(pl.multiple_of(col * LANES, LANES), LANES),
                    ] = piece.astype(BF16)
            return carry

        lax.fori_loop(0, 2 * COLS // 4, order, 0)
        weights = jnp.concatenate(
            [flat[pl.ds(2 * CAP * COLS + j, SRC, stride=FROWS), :] for j in range(CAP)], axis=0
        )
        weights = jnp.concatenate([weights, weights], axis=1)
        xs = rows[pl.ds(base, ROWS), 0:FEAT]
        dys = rows[pl.ds(base, ROWS), FEAT : 2 * FEAT]
        gate = jnp.dot(xs, wg[...], preferred_element_type=F32)
        up = jnp.dot(xs, wu[...], preferred_element_type=F32)
        proj = lax.dot_general(dys, wd[...], (((1,), (1,)), ((), ())), preferred_element_type=F32)
        sig = jax.nn.sigmoid(gate)
        hidden = (gate * sig * up).astype(BF16).astype(F32)
        route = jnp.sum(hidden * proj, axis=1, keepdims=True)
        scaled = weights * proj
        d_gate = (scaled * up * sig * (1.0 + gate * (1.0 - sig))).astype(BF16)
        d_up = (scaled * gate * sig).astype(BF16)
        dgu[pl.ds(base, ROWS), 0:HID] = d_gate
        dgu[pl.ds(base, ROWS), HID : 2 * HID] = d_up
        wtd[pl.ds(base, ROWS), :] = (weights * hidden).astype(BF16)
        lane = lax.broadcasted_iota(jnp.int32, (SRC, LANES), 1)
        line = jnp.zeros((SRC, LANES), F32)
        for j in range(CAP):
            line = line + jnp.where(lane == j, route[j * SRC : (j + 1) * SRC, :], 0.0)
        retf[pl.ds(CAP * COLS, SRC, stride=RROWS), :] = line

        def spread(m, carry):
            cols = pl.ds(pl.multiple_of(m * 256, 256), 256)
            nt = (((1,), (1,)), ((), ()))
            dg = dgu[pl.ds(base, ROWS), 0:HID]
            du = dgu[pl.ds(base, ROWS), HID : 2 * HID]
            piece = lax.dot_general(dg, wg[cols, :], nt, preferred_element_type=F32)
            piece = piece + lax.dot_general(du, wu[cols, :], nt, preferred_element_type=F32)
            for h in range(2):
                for j in range(CAP):
                    retf[pl.ds(j * COLS + m * 2 + h, SRC, stride=RROWS), :] = piece[
                        j * SRC : (j + 1) * SRC, h * LANES : (h + 1) * LANES
                    ]
            return carry

        lax.fori_loop(0, FEAT // 256, spread, 0)
        size = 2 * STEP * RROWS
        pst[g] = retf[pl.ds(pl.multiple_of((1 - c) * size, 8), size), :].astype(BF16)
        part(g).start()
        own[g] = retf[pl.ds(pl.multiple_of(c * size, 8), size), :].astype(BF16)

    def reply(g):
        part(g).wait_recv()
        rsend[g] = (own[g].astype(F32) + prt[g].astype(F32)).astype(BF16)

    def local(g):
        return pltpu.make_async_copy(
            rsend.at[0, pl.ds(pl.multiple_of(xl * RROWS, 16), RROWS)], ret.at[0, xl * STEP], ret_sem.at[0]
        )

    take(0)

    def chunk(g, carry):
        @pl.when(g < CHUNKS - 1)
        def _():
            take(g + 1)

        forward(g).wait_recv()
        compute(g)

        @pl.when(g == 1)
        def _():
            reply(0)
            local(0).start()
            back(0, 0, 1 - xl).start()
            for i in range(2, 2 * STEP):
                back(0, i, i % 2).start()

        @pl.when(g > 1)
        def _():
            reply(g - 1)
            for i in range(2 * STEP):
                back(g - 1, i, i % 2).start()

        return carry

    lax.fori_loop(0, CHUNKS, chunk, 0)
    reply(CHUNKS - 1)
    for i in range(2 * STEP):
        back(CHUNKS - 1, i, i % 2).start()

    tn = (((0,), (0,)), ((), ()))

    def grads(m, carry):
        at = pl.ds(pl.multiple_of(m * 256, 256), 256)
        far = pl.ds(pl.multiple_of(FEAT + m * 256, 256), 256)
        both = lax.dot_general(rows[:, at], dgu[...], tn, preferred_element_type=F32)
        sg[at, :] = both[:, 0:HID].astype(BF16)
        su[at, :] = both[:, HID : 2 * HID].astype(BF16)
        down = lax.dot_general(wtd[...], rows[:, far], tn, preferred_element_type=F32)
        sd[:, at] = down.astype(BF16)
        return carry

    lax.fori_loop(0, FEAT // 256, grads, 0)
    stores = [
        pltpu.make_async_copy(v, h, out_sem.at[i])
        for i, (h, v) in enumerate(((gg_hbm, sg), (gu_hbm, su), (gd_hbm, sd)))
    ]
    for copy in stores:
        copy.start()

    def collect(g, carry):
        pltpu.make_async_copy(ret.at[g], ret.at[g], ret_sem.at[g]).wait()
        for xs in range(2):
            for kq in range(STEP):
                at = (xs * EXP + g * STEP + kq) * RROWS
                flat[pl.ds(pl.multiple_of(at, 8), RROWS), :] = ret[g, xs * STEP + kq].astype(F32)
        return carry

    lax.fori_loop(0, CHUNKS, collect, 0)

    def merge(q, carry):
        for h in range(2):
            col = q * 2 + h
            for j in range(CAP):
                near = flat[pl.ds(j * COLS + col, EXP, stride=RROWS), :]
                far = flat[pl.ds(EXP * RROWS + j * COLS + col, EXP, stride=RROWS), :]
                got[j * EXP : (j + 1) * EXP, pl.ds(pl.multiple_of(col * LANES, LANES), LANES)] = (
                    near + far
                ).astype(BF16)
        return carry

    lax.fori_loop(0, COLS // 2, merge, 0)
    line = (
        flat[pl.ds(CAP * COLS, EXP, stride=RROWS), :]
        + flat[pl.ds(EXP * RROWS + CAP * COLS, EXP, stride=RROWS), :]
    )
    spot = jnp.zeros((EXP, TOK), F32)
    for j in range(CAP):
        spot = spot + slots[j * EXP : (j + 1) * EXP, :].astype(F32) * line[:, j : j + 1]
    for q in range(8):
        gr_ref[q : q + 1, :] = jnp.sum(
            jnp.where(ids_ref[q : q + 1, :] == target, spot, 0.0), axis=0, keepdims=True
        )

    def place(m, carry):
        at = pl.ds(pl.multiple_of(m * 512, 512), 512)
        gt_ref[:, at] = lax.dot_general(slots[...], got[:, at], tn, preferred_element_type=F32).astype(BF16)
        return carry

    lax.fori_loop(0, FEAT // 512, place, 0)

    for copy in stores:
        copy.wait()
    remote(0, 1 - xl).wait_send()
    back(0, 0, 1 - xl).wait_send()

    def drain(k, carry):
        remote(k, 0).wait_send()
        remote(k, 1).wait_send()
        return carry

    lax.fori_loop(1, EXP, drain, 0)

    def drain_back(i, carry):
        pltpu.make_async_copy(
            rsend.at[0, pl.ds(0, RROWS)], rsend.at[0, pl.ds(0, RROWS)], rs_sem.at[i]
        ).wait()
        return carry

    lax.fori_loop(2, CHUNKS * 2 * STEP, drain_back, 0)

    def drain_pairs(g, carry):
        forward(g).wait_send()
        part(g).wait_send()
        return carry

    lax.fori_loop(0, CHUNKS, drain_pairs, 0)


def shards(tokens, out_grad, expert_ids, route_weights, w_gate, w_up, w_down):
    vmem = pl.BlockSpec(memory_space=pltpu.VMEM)
    anywhere = pl.BlockSpec(memory_space=pl.ANY)
    size = 2 * STEP * RROWS
    dma = pltpu.SemaphoreType.DMA
    grad_tokens, grad_route, grad_g, grad_u, grad_d = pl.pallas_call(
        body,
        out_shape=(
            jax.ShapeDtypeStruct((TOK, FEAT), BF16),
            jax.ShapeDtypeStruct((8, TOK), F32),
            jax.ShapeDtypeStruct((FEAT, HID), BF16),
            jax.ShapeDtypeStruct((FEAT, HID), BF16),
            jax.ShapeDtypeStruct((HID, FEAT), BF16),
        ),
        in_specs=[vmem, vmem, vmem, vmem, anywhere, anywhere, anywhere],
        out_specs=(vmem, vmem, anywhere, anywhere, anywhere),
        scratch_shapes=[
            pltpu.VMEM((FEAT, HID), BF16),
            pltpu.VMEM((FEAT, HID), BF16),
            pltpu.VMEM((HID, FEAT), BF16),
            pltpu.VMEM((EXP * FROWS, LANES), F32),
            pltpu.VMEM((EXP, FROWS, LANES), BF16),
            pltpu.VMEM((CHUNKS, SRC, FROWS, LANES), BF16),
            pltpu.VMEM((ALL, 2 * FEAT), BF16),
            pltpu.VMEM((ALL, 2 * HID), BF16),
            pltpu.VMEM((ALL, HID), BF16),
            pltpu.VMEM((SRC * RROWS, LANES), F32),
            pltpu.VMEM((CHUNKS, size, LANES), BF16),
            pltpu.VMEM((CHUNKS, size, LANES), BF16),
            pltpu.VMEM((CHUNKS, size, LANES), BF16),
            pltpu.VMEM((CHUNKS, size, LANES), BF16),
            pltpu.VMEM((CHUNKS, 2 * STEP, RROWS, LANES), BF16),
            pltpu.VMEM((CAP * EXP, TOK), BF16),
            pltpu.VMEM((CAP * EXP, FEAT), BF16),
            pltpu.VMEM((FEAT, HID), BF16),
            pltpu.VMEM((FEAT, HID), BF16),
            pltpu.VMEM((HID, FEAT), BF16),
            dma((2 * EXP,)),
            dma((CHUNKS,)),
            dma((CHUNKS,)),
            dma((CHUNKS,)),
            dma((CHUNKS,)),
            dma((CHUNKS,)),
            dma((2 * EXP,)),
            dma((CHUNKS,)),
            dma((3,)),
            dma((3,)),
        ],
        compiler_params=pltpu.CompilerParams(has_side_effects=True, vmem_limit_bytes=63_000_000),
    )(
        expert_ids.T,
        route_weights.astype(F32).T,
        tokens,
        out_grad,
        w_gate[0],
        w_up[0],
        w_down[0],
    )
    return (grad_tokens, grad_route.T.astype(BF16), grad_g[None], grad_u[None], grad_d[None])


def solution(mesh):
    rows_spec = P(("expert", "dp"), None)
    hidden_last = P("expert", None, "dp")
    hidden_mid = P("expert", "dp", None)
    return jax.shard_map(
        shards,
        mesh=mesh,
        in_specs=(rows_spec,) * 4 + (hidden_last, hidden_last, hidden_mid),
        out_specs=(rows_spec, rows_spec, hidden_last, hidden_last, hidden_mid),
        check_vma=False,
    )
```

```python
import jax
import jax.numpy as jnp
from jax import lax
from jax.experimental import pallas as pl
from jax.experimental.pallas import tpu as pltpu
from jax.sharding import PartitionSpec as P

NZ, NY, NX = 4, 4, 2
EXP = NZ * NY * NX
CAP = 5
STEP = 4
CHUNKS = EXP // STEP
LANES = 128
FEAT = 3584
HID = 256
COLS = FEAT // LANES
FROWS = 288
RROWS = 144
SRC = 4 * STEP
ROWS = SRC * CAP
ALL = ROWS * CHUNKS
TOK = 128
MESH = pl.DeviceIdType.MESH
F32, BF16 = jnp.float32, jnp.bfloat16


def steps(k):
    kz = k & 3
    return kz, (kz + (k >> 2)) & 3, (kz + (k >> 4)) & 1


def shifted(e, k, sign):
    z, y, x = e // (NY * NX), (e // NX) % NY, e % NX
    kz, ky, kx = steps(k)
    z = (z + NZ + sign * kz) & 3
    y = (y + NY + sign * ky) & 3
    x = (x + NX + sign * kx) & 1
    return (z * NY + y) * NX + x


def body(
    ids_ref, rw_ref, tok_ref, dy_ref, wg_hbm, wu_hbm, wd_hbm,
    gt_ref, gr_ref, sg, su, sd,
    wg, wu, wd, flat, send, recv, rows, dgu, wtd, retf, own, pst, prt, rsend, ret, slots, early, got,
    send_sem, recv_sem, fws_sem, fwr_sem, pas_sem, par_sem, rs_sem, ret_sem, win_sem,
):
    e = lax.axis_index("expert")
    d = lax.axis_index("dp")
    xl, c = d // 2, d % 2
    partner = {"expert": e, "dp": xl * 2 + 1 - c}

    barrier = pltpu.get_barrier_semaphore()

    def greet(k, xd):
        there = {"expert": shifted(e, k, 1), "dp": xd * 2 + c}
        pl.semaphore_signal(barrier, inc=1, device_id=there, device_id_type=MESH)

    def greet_both(k, carry):
        greet(k, 0)
        greet(k, 1)
        return carry

    greet(0, 1 - xl)
    pl.semaphore_signal(barrier, inc=1, device_id=partner, device_id_type=MESH)
    lax.fori_loop(1, EXP, greet_both, 0)

    loads = [
        pltpu.make_async_copy(h, v, win_sem.at[i])
        for i, (h, v) in enumerate(((wg_hbm, wg), (wu_hbm, wu), (wd_hbm, wd)))
    ]
    for copy in loads:
        copy.start()

    kk = lax.broadcasted_iota(jnp.int32, (EXP, TOK), 0)
    z, y, x = e // (NY * NX), (e // NX) % NY, e % NX
    kz, ky, kx = steps(kk)
    tz, ty, tx = (z + kz) & 3, (y + ky) & 3, (x + kx) & 1
    target = tz * (NY * NX) + ty * NX + tx
    chosen = jnp.zeros((EXP, TOK), F32)
    weight = jnp.zeros((EXP, TOK), F32)
    rw = rw_ref[...].astype(F32)
    for q in range(8):
        same = ids_ref[q : q + 1, :] == target
        chosen = chosen + jnp.where(same, 1.0, 0.0)
        weight = weight + jnp.where(same, rw[q : q + 1, :], 0.0)
    before = lax.broadcasted_iota(jnp.int32, (TOK, TOK), 0) < lax.broadcasted_iota(
        jnp.int32, (TOK, TOK), 1
    )
    rank = jnp.dot(
        chosen.astype(BF16), jnp.where(before, 1.0, 0.0).astype(BF16), preferred_element_type=F32
    )
    for j in range(CAP):
        hot = jnp.where(jnp.abs(rank - j) < 0.5, chosen, 0.0)
        slots[j * EXP : (j + 1) * EXP, :] = hot.astype(BF16)
        for p in range(EXP // 8):
            early[p, j * 8 : (j + 1) * 8, :] = hot[p * 8 : (p + 1) * 8, :]
        one = jnp.sum(hot * weight, axis=1, keepdims=True)
        flat[pl.ds(2 * CAP * COLS + j, EXP, stride=FROWS), :] = jnp.broadcast_to(one, (EXP, LANES))
    for j in range(2 * CAP * COLS + CAP, FROWS):
        flat[pl.ds(j, EXP, stride=FROWS), :] = jnp.zeros((EXP, LANES), F32)
    for j in range(CAP * COLS + 1, RROWS):
        retf[pl.ds(j, SRC, stride=RROWS), :] = jnp.zeros((SRC, LANES), F32)

    def remote(k, xd):
        g, kq = k // STEP, k % STEP
        return pltpu.make_async_remote_copy(
            src_ref=send.at[k],
            dst_ref=recv.at[g, c * (2 * STEP) + kq * 2 + xl],
            send_sem=send_sem.at[k * 2 + xd],
            recv_sem=recv_sem.at[g],
            device_id={"expert": shifted(e, k, 1), "dp": xd * 2 + c},
            device_id_type=MESH,
        )

    def pack(k):
        send[k] = flat[pl.ds(pl.multiple_of(k * FROWS, 8), FROWS), :].astype(BF16)

    def issue(k, carry):
        pack(k)
        remote(k, 0).start()
        remote(k, 1).start()
        return carry

    def pick(p):
        hots = early[p].astype(BF16)

        def gather(m, carry):
            for a, ref in enumerate((tok_ref, dy_ref)):
                picked = jnp.dot(
                    hots, ref[:, pl.ds(pl.multiple_of(m * 256, 256), 256)], preferred_element_type=F32
                )
                for h in range(2):
                    for j in range(CAP):
                        at = p * 8 * FROWS + j * 2 * COLS + a * COLS + m * 2 + h
                        flat[pl.ds(at, 8, stride=FROWS), :] = picked[
                            j * 8 : (j + 1) * 8, h * LANES : (h + 1) * LANES
                        ]
            return carry

        lax.fori_loop(0, FEAT // 256, gather, 0)

    pick(0)
    pack(0)
    pl.semaphore_wait(barrier, 2 * EXP)
    remote(0, 1 - xl).start()
    pltpu.make_async_copy(send.at[0], recv.at[0, c * (2 * STEP) + xl], recv_sem.at[0]).start()
    lax.fori_loop(1, 8, issue, 0)

    def later(p, carry):
        pick(p)
        lax.fori_loop(p * 8, p * 8 + 8, issue, 0)
        return carry

    lax.fori_loop(1, EXP // 8, later, 0)
    for copy in loads:
        copy.wait()

    def half(g, core):
        return recv.at[g, pl.ds(core * (2 * STEP), 2 * STEP)]

    def forward(g):
        return pltpu.make_async_remote_copy(
            src_ref=half(g, c), dst_ref=half(g, c), send_sem=fws_sem.at[g], recv_sem=fwr_sem.at[g],
            device_id=partner, device_id_type=MESH,
        )

    def take(g):
        pltpu.make_async_copy(half(g, c), half(g, c), recv_sem.at[g]).wait()
        forward(g).start()

    def part(g):
        return pltpu.make_async_remote_copy(
            src_ref=pst.at[g], dst_ref=prt.at[g], send_sem=pas_sem.at[g], recv_sem=par_sem.at[g],
            device_id=partner, device_id_type=MESH,
        )

    def back(g, i, xs):
        kq = i // 2
        return pltpu.make_async_remote_copy(
            src_ref=rsend.at[g, pl.ds(pl.multiple_of((kq * 2 + xs) * RROWS, 16), RROWS)],
            dst_ref=ret.at[g, xl * STEP + kq],
            send_sem=rs_sem.at[g * (2 * STEP) + i],
            recv_sem=ret_sem.at[g],
            device_id={"expert": shifted(e, g * STEP + kq, -1), "dp": xs * 2 + c},
            device_id_type=MESH,
        )

    def compute(g):
        def widen(s, carry):
            flat[pl.ds(pl.multiple_of(s * FROWS, 8), FROWS), :] = recv[g, s].astype(F32)
            return carry

        lax.fori_loop(0, SRC, widen, 0)
        base = pl.multiple_of(g * ROWS, 16)

        def order(q, carry):
            for h in range(4):
                col = q * 4 + h
                for j in range(CAP):
                    piece = flat[pl.ds(j * 2 * COLS + col, SRC, stride=FROWS), :]
                    rows[
                        pl.ds(pl.multiple_of(base + j * SRC, 16), SRC),
                        pl.ds(pl.multiple_of(col * LANES, LANES), LANES),
                    ] = piece.astype(BF16)
            return carry

        lax.fori_loop(0, 2 * COLS // 4, order, 0)
        weights = jnp.concatenate(
            [flat[pl.ds(2 * CAP * COLS + j, SRC, stride=FROWS), :] for j in range(CAP)], axis=0
        )
        weights = jnp.concatenate([weights, weights], axis=1)
        xs = rows[pl.ds(base, ROWS), 0:FEAT]
        dys = rows[pl.ds(base, ROWS), FEAT : 2 * FEAT]
        gate = jnp.dot(xs, wg[...], preferred_element_type=F32)
        up = jnp.dot(xs, wu[...], preferred_element_type=F32)
        proj = lax.dot_general(dys, wd[...], (((1,), (1,)), ((), ())), preferred_element_type=F32)
        sig = jax.nn.sigmoid(gate)
        hidden = (gate * sig * up).astype(BF16).astype(F32)
        route = jnp.sum(hidden * proj, axis=1, keepdims=True)
        scaled = weights * proj
        d_gate = (scaled * up * sig * (1.0 + gate * (1.0 - sig))).astype(BF16)
        d_up = (scaled * gate * sig).astype(BF16)
        dgu[pl.ds(base, ROWS), 0:HID] = d_gate
        dgu[pl.ds(base, ROWS), HID : 2 * HID] = d_up
        wtd[pl.ds(base, ROWS), :] = (weights * hidden).astype(BF16)
        lane = lax.broadcasted_iota(jnp.int32, (SRC, LANES), 1)
        line = jnp.zeros((SRC, LANES), F32)
        for j in range(CAP):
            line = line + jnp.where(lane == j, route[j * SRC : (j + 1) * SRC, :], 0.0)
        retf[pl.ds(CAP * COLS, SRC, stride=RROWS), :] = line

        def spread(m, carry):
            cols = pl.ds(pl.multiple_of(m * 256, 256), 256)
            nt = (((1,), (1,)), ((), ()))
            dg = dgu[pl.ds(base, ROWS), 0:HID]
            du = dgu[pl.ds(base, ROWS), HID : 2 * HID]
            piece = lax.dot_general(dg, wg[cols, :], nt, preferred_element_type=F32)
            piece = piece + lax.dot_general(du, wu[cols, :], nt, preferred_element_type=F32)
            for h in range(2):
                for j in range(CAP):
                    retf[pl.ds(j * COLS + m * 2 + h, SRC, stride=RROWS), :] = piece[
                        j * SRC : (j + 1) * SRC, h * LANES : (h + 1) * LANES
                    ]
            return carry

        lax.fori_loop(0, FEAT // 256, spread, 0)
        size = 2 * STEP * RROWS
        pst[g] = retf[pl.ds(pl.multiple_of((1 - c) * size, 8), size), :].astype(BF16)
        part(g).start()
        own[g] = retf[pl.ds(pl.multiple_of(c * size, 8), size), :].astype(BF16)

    def reply(g):
        part(g).wait_recv()
        rsend[g] = (own[g].astype(F32) + prt[g].astype(F32)).astype(BF16)

    def local(g):
        return pltpu.make_async_copy(
            rsend.at[0, pl.ds(pl.multiple_of(xl * RROWS, 16), RROWS)], ret.at[0, xl * STEP], ret_sem.at[0]
        )

    take(0)

    def chunk(g, carry):
        @pl.when(g < CHUNKS - 1)
        def _():
            take(g + 1)

        forward(g).wait_recv()
        compute(g)

        @pl.when(g == 1)
        def _():
            reply(0)
            local(0).start()
            back(0, 0, 1 - xl).start()
            for i in range(2, 2 * STEP):
                back(0, i, i % 2).start()

        @pl.when(g > 1)
        def _():
            reply(g - 1)
            for i in range(2 * STEP):
                back(g - 1, i, i % 2).start()

        return carry

    lax.fori_loop(0, CHUNKS, chunk, 0)
    reply(CHUNKS - 1)
    for i in range(2 * STEP):
        back(CHUNKS - 1, i, i % 2).start()

    tn = (((0,), (0,)), ((), ()))

    def grads(m, carry):
        at = pl.ds(pl.multiple_of(m * 256, 256), 256)
        far = pl.ds(pl.multiple_of(FEAT + m * 256, 256), 256)
        both = lax.dot_general(rows[:, at], dgu[...], tn, preferred_element_type=F32)
        sg[at, :] = both[:, 0:HID].astype(BF16)
        su[at, :] = both[:, HID : 2 * HID].astype(BF16)
        down = lax.dot_general(wtd[...], rows[:, far], tn, preferred_element_type=F32)
        sd[:, at] = down.astype(BF16)
        return carry

    lax.fori_loop(0, FEAT // 256, grads, 0)
    def collect(g, carry):
        pltpu.make_async_copy(ret.at[g], ret.at[g], ret_sem.at[g]).wait()
        for xs in range(2):
            for kq in range(STEP):
                at = (xs * EXP + g * STEP + kq) * RROWS
                flat[pl.ds(pl.multiple_of(at, 8), RROWS), :] = ret[g, xs * STEP + kq].astype(F32)
        return carry

    lax.fori_loop(0, CHUNKS, collect, 0)

    def merge(q, carry):
        for h in range(2):
            col = q * 2 + h
            for j in range(CAP):
                near = flat[pl.ds(j * COLS + col, EXP, stride=RROWS), :]
                far = flat[pl.ds(EXP * RROWS + j * COLS + col, EXP, stride=RROWS), :]
                got[j * EXP : (j + 1) * EXP, pl.ds(pl.multiple_of(col * LANES, LANES), LANES)] = (
                    near + far
                ).astype(BF16)
        return carry

    lax.fori_loop(0, COLS // 2, merge, 0)
    line = (
        flat[pl.ds(CAP * COLS, EXP, stride=RROWS), :]
        + flat[pl.ds(EXP * RROWS + CAP * COLS, EXP, stride=RROWS), :]
    )
    spot = jnp.zeros((EXP, TOK), F32)
    for j in range(CAP):
        spot = spot + slots[j * EXP : (j + 1) * EXP, :].astype(F32) * line[:, j : j + 1]
    for q in range(8):
        gr_ref[q : q + 1, :] = jnp.sum(
            jnp.where(ids_ref[q : q + 1, :] == target, spot, 0.0), axis=0, keepdims=True
        ).astype(BF16)

    def place(m, carry):
        at = pl.ds(pl.multiple_of(m * 512, 512), 512)
        gt_ref[:, at] = lax.dot_general(slots[...], got[:, at], tn, preferred_element_type=F32).astype(BF16)
        return carry

    lax.fori_loop(0, FEAT // 512, place, 0)

    remote(0, 1 - xl).wait_send()
    back(0, 0, 1 - xl).wait_send()

    def drain(k, carry):
        remote(k, 0).wait_send()
        remote(k, 1).wait_send()
        return carry

    lax.fori_loop(1, EXP, drain, 0)

    def drain_back(i, carry):
        pltpu.make_async_copy(
            rsend.at[0, pl.ds(0, RROWS)], rsend.at[0, pl.ds(0, RROWS)], rs_sem.at[i]
        ).wait()
        return carry

    lax.fori_loop(2, CHUNKS * 2 * STEP, drain_back, 0)

    def drain_pairs(g, carry):
        forward(g).wait_send()
        part(g).wait_send()
        return carry

    lax.fori_loop(0, CHUNKS, drain_pairs, 0)


def shards(tokens, out_grad, expert_ids, route_weights, w_gate, w_up, w_down):
    vmem = pl.BlockSpec(memory_space=pltpu.VMEM)
    anywhere = pl.BlockSpec(memory_space=pl.ANY)
    size = 2 * STEP * RROWS
    dma = pltpu.SemaphoreType.DMA
    shapes = ((TOK, FEAT), (8, TOK), (FEAT, HID), (FEAT, HID), (HID, FEAT))
    made = pl.pallas_call(
        body,
        out_shape=tuple(pltpu.VMEM(s, BF16) for s in shapes),
        in_specs=[vmem, vmem, vmem, vmem, anywhere, anywhere, anywhere],
        out_specs=(vmem,) * 5,
        scratch_shapes=[
            pltpu.VMEM((FEAT, HID), BF16),
            pltpu.VMEM((FEAT, HID), BF16),
            pltpu.VMEM((HID, FEAT), BF16),
            pltpu.VMEM((EXP * FROWS, LANES), F32),
            pltpu.VMEM((EXP, FROWS, LANES), BF16),
            pltpu.VMEM((CHUNKS, SRC, FROWS, LANES), BF16),
            pltpu.VMEM((ALL, 2 * FEAT), BF16),
            pltpu.VMEM((ALL, 2 * HID), BF16),
            pltpu.VMEM((ALL, HID), BF16),
            pltpu.VMEM((SRC * RROWS, LANES), F32),
            pltpu.VMEM((CHUNKS, size, LANES), BF16),
            pltpu.VMEM((CHUNKS, size, LANES), BF16),
            pltpu.VMEM((CHUNKS, size, LANES), BF16),
            pltpu.VMEM((CHUNKS, size, LANES), BF16),
            pltpu.VMEM((CHUNKS, 2 * STEP, RROWS, LANES), BF16),
            pltpu.VMEM((CAP * EXP, TOK), BF16),
            pltpu.VMEM((EXP // 8, CAP * 8, TOK), F32),
            pltpu.VMEM((CAP * EXP, FEAT), BF16),
            dma((2 * EXP,)),
            dma((CHUNKS,)),
            dma((CHUNKS,)),
            dma((CHUNKS,)),
            dma((CHUNKS,)),
            dma((CHUNKS,)),
            dma((2 * EXP,)),
            dma((CHUNKS,)),
            dma((3,)),
        ],
        compiler_params=pltpu.CompilerParams(
            collective_id=0, has_side_effects=True, vmem_limit_bytes=50_000_000
        ),
    )(
        expert_ids.T,
        route_weights.T,
        tokens,
        out_grad,
        w_gate[0],
        w_up[0],
        w_down[0],
    )
    grad_tokens, grad_route, grad_g, grad_u, grad_d = made
    return (grad_tokens, grad_route.T, grad_g[None], grad_u[None], grad_d[None])


def solution(mesh):
    rows_spec = P(("expert", "dp"), None)
    hidden_last = P("expert", None, "dp")
    hidden_mid = P("expert", "dp", None)
    return jax.shard_map(
        shards,
        mesh=mesh,
        in_specs=(rows_spec,) * 4 + (hidden_last, hidden_last, hidden_mid),
        out_specs=(rows_spec, rows_spec, hidden_last, hidden_last, hidden_mid),
        check_vma=False,
    )
```

```python
import jax
import jax.numpy as jnp
from jax import lax
from jax.experimental import pallas as pl
from jax.experimental.pallas import tpu as pltpu
from jax.sharding import PartitionSpec as P

NZ, NY, NX = 4, 4, 2
EXP = NZ * NY * NX
CAP = 5
STEP = 4
CHUNKS = EXP // STEP
LANES = 128
FEAT = 3584
HID = 256
COLS = FEAT // LANES
FROWS = 288
RROWS = 144
FPITCH, RPITCH = FROWS + 1, RROWS + 1
SRC = 4 * STEP
ROWS = SRC * CAP
ALL = ROWS * CHUNKS
SPAN = 3 * ROWS
TOK = 128
MESH = pl.DeviceIdType.MESH
F32, BF16 = jnp.float32, jnp.bfloat16


def steps(k):
    kz = k & 3
    return kz, (kz + (k >> 2)) & 3, (kz + (k >> 4)) & 1


def shifted(e, k, sign):
    z, y, x = e >> 3, (e >> 1) & 3, e & 1
    kz, ky, kx = steps(k)
    z = (z + NZ + sign * kz) & 3
    y = (y + NY + sign * ky) & 3
    x = (x + NX + sign * kx) & 1
    return (z << 3) + (y << 1) + x


def targets(e):
    z, y, x = e >> 3, (e >> 1) & 3, e & 1
    kz, ky, kx = steps(lax.broadcasted_iota(jnp.int32, (EXP, TOK), 0))
    return (((z + kz) & 3) << 3) + (((y + ky) & 3) << 1) + ((x + kx) & 1)


def body(
    ids_ref, rw_ref, tok_ref, dy_ref, wg_hbm, wu_hbm, wd_hbm,
    flat, slots, sg, su, sd,
    wgu, wgut, wd, send, recv, rows, dgu, wtd, retf, own, pst, prt, rsend, ret, early,
    send_sem, recv_sem, fws_sem, fwr_sem, pas_sem, par_sem, rs_sem, ret_sem, win_sem,
):
    e = lax.axis_index("expert")
    d = lax.axis_index("dp")
    xl, c = d >> 1, d & 1
    partner = {"expert": e, "dp": xl * 2 + 1 - c}

    barrier = pltpu.get_barrier_semaphore()

    def greet(k, xd):
        there = {"expert": shifted(e, k, 1), "dp": xd * 2 + c}
        pl.semaphore_signal(barrier, inc=1, device_id=there, device_id_type=MESH)

    def greet_both(k, carry):
        greet(k, 0)
        greet(k, 1)
        return carry

    greet(0, 1 - xl)
    pl.semaphore_signal(barrier, inc=1, device_id=partner, device_id_type=MESH)
    lax.fori_loop(1, EXP, greet_both, 0)

    loads = [
        pltpu.make_async_copy(h, v, win_sem.at[i])
        for i, (h, v) in enumerate(((wg_hbm, wgu.at[:, 0:HID]), (wu_hbm, wgu.at[:, HID : 2 * HID]), (wd_hbm, wd)))
    ]
    for copy in loads:
        copy.start()

    target = targets(e)
    chosen = jnp.zeros((EXP, TOK), F32)
    weight = jnp.zeros((EXP, TOK), F32)
    rw = rw_ref[...].astype(F32)
    for q in range(8):
        same = ids_ref[q : q + 1, :] == target
        chosen = chosen + jnp.where(same, 1.0, 0.0)
        weight = weight + jnp.where(same, rw[q : q + 1, :], 0.0)
    before = lax.broadcasted_iota(jnp.int32, (TOK, TOK), 0) < lax.broadcasted_iota(
        jnp.int32, (TOK, TOK), 1
    )
    rank = jnp.dot(
        chosen.astype(BF16), jnp.where(before, 1.0, 0.0).astype(BF16), preferred_element_type=F32
    )
    for j in range(CAP):
        hot = jnp.where(jnp.abs(rank - j) < 0.5, chosen, 0.0)
        slots[j * EXP : (j + 1) * EXP, :] = hot.astype(BF16)
        for p in range(EXP // 8):
            early[p, j * 8 : (j + 1) * 8, :] = hot[p * 8 : (p + 1) * 8, :]
        one = jnp.sum(hot * weight, axis=1, keepdims=True)
        flat[pl.ds(2 * CAP * COLS + j, EXP, stride=FPITCH), :] = jnp.broadcast_to(one, (EXP, LANES))
    for j in range(2 * CAP * COLS + CAP, FROWS):
        flat[pl.ds(j, EXP, stride=FPITCH), :] = jnp.zeros((EXP, LANES), F32)
    for j in range(CAP * COLS + 1, RROWS):
        retf[pl.ds(j, SRC, stride=RPITCH), :] = jnp.zeros((SRC, LANES), F32)

    def remote(k, xd):
        g, kq = k >> 2, k & 3
        return pltpu.make_async_remote_copy(
            src_ref=send.at[k],
            dst_ref=recv.at[g, c * (2 * STEP) + kq * 2 + xl],
            send_sem=send_sem.at[k * 2 + xd],
            recv_sem=recv_sem.at[g],
            device_id={"expert": shifted(e, k, 1), "dp": xd * 2 + c},
            device_id_type=MESH,
        )

    def pack(k):
        send[k] = flat[pl.ds(k * FPITCH, FROWS), :].astype(BF16)

    def issue(k, carry):
        pack(k)
        remote(k, 0).start()
        remote(k, 1).start()
        return carry

    def pick(p):
        hots = early[p].astype(BF16)

        def gather(m, carry):
            for a, ref in enumerate((tok_ref, dy_ref)):
                picked = jnp.dot(
                    hots, ref[:, pl.ds(pl.multiple_of(m * 512, 512), 512)], preferred_element_type=F32
                )
                for h in range(4):
                    for j in range(CAP):
                        at = p * 8 * FPITCH + j * 2 * COLS + a * COLS + m * 4 + h
                        flat[pl.ds(at, 8, stride=FPITCH), :] = picked[
                            j * 8 : (j + 1) * 8, h * LANES : (h + 1) * LANES
                        ]
            return carry

        lax.fori_loop(0, FEAT // 512, gather, 0)

    pick(0)
    pack(0)
    pl.semaphore_wait(barrier, 2 * EXP)
    remote(0, 1 - xl).start()
    pltpu.make_async_copy(send.at[0], recv.at[0, c * (2 * STEP) + xl], recv_sem.at[0]).start()
    lax.fori_loop(1, 8, issue, 0)

    def later(p, carry):
        pick(p)
        lax.fori_loop(p * 8, p * 8 + 8, issue, 0)
        return carry

    lax.fori_loop(1, EXP // 8, later, 0)
    for copy in loads:
        copy.wait()

    def turn(m, carry):
        at = pl.ds(pl.multiple_of(m * 512, 512), 512)
        wgut[:, at] = wgu[at, :].T
        return carry

    lax.fori_loop(0, FEAT // 512, turn, 0)

    def half(g, core):
        return recv.at[g, pl.ds(core * (2 * STEP), 2 * STEP)]

    def forward(g):
        return pltpu.make_async_remote_copy(
            src_ref=half(g, c), dst_ref=half(g, c), send_sem=fws_sem.at[g], recv_sem=fwr_sem.at[g],
            device_id=partner, device_id_type=MESH,
        )

    def take(g):
        pltpu.make_async_copy(half(g, c), half(g, c), recv_sem.at[g]).wait()
        forward(g).start()

    def part(g):
        return pltpu.make_async_remote_copy(
            src_ref=pst.at[g], dst_ref=prt.at[g], send_sem=pas_sem.at[g], recv_sem=par_sem.at[g],
            device_id=partner, device_id_type=MESH,
        )

    def back(g, i, xs):
        kq = i // 2
        return pltpu.make_async_remote_copy(
            src_ref=rsend.at[g, pl.ds(pl.multiple_of((kq * 2 + xs) * RROWS, 16), RROWS)],
            dst_ref=ret.at[g, xl * STEP + kq],
            send_sem=rs_sem.at[g * (2 * STEP) + i],
            recv_sem=ret_sem.at[g],
            device_id={"expert": shifted(e, g * STEP + kq, -1), "dp": xs * 2 + c},
            device_id_type=MESH,
        )

    def compute(g):
        def widen(s, carry):
            flat[pl.ds(s * FPITCH, FROWS), :] = recv[g, s].astype(F32)
            return carry

        lax.fori_loop(0, SRC, widen, 0)
        base = pl.multiple_of(g * ROWS, 16)

        def order(q, carry):
            for h in range(4):
                col = q * 4 + h
                for j in range(CAP):
                    piece = flat[pl.ds(j * 2 * COLS + col, SRC, stride=FPITCH), :]
                    rows[
                        pl.ds(pl.multiple_of(base + j * SRC, 16), SRC),
                        pl.ds(pl.multiple_of(col * LANES, LANES), LANES),
                    ] = piece.astype(BF16)
            return carry

        lax.fori_loop(0, 2 * COLS // 4, order, 0)
        weights = jnp.concatenate(
            [flat[pl.ds(2 * CAP * COLS + j, SRC, stride=FPITCH), :] for j in range(CAP)], axis=0
        )
        weights = jnp.concatenate([weights, weights], axis=1)
        xs = rows[pl.ds(base, ROWS), 0:FEAT]
        dys = rows[pl.ds(base, ROWS), FEAT : 2 * FEAT]
        both = jnp.dot(xs, wgu[...], preferred_element_type=F32)
        gate, up = both[:, 0:HID], both[:, HID : 2 * HID]
        proj = lax.dot_general(dys, wd[...], (((1,), (1,)), ((), ())), preferred_element_type=F32)
        sig = jax.nn.sigmoid(gate)
        hidden = (gate * sig * up).astype(BF16).astype(F32)
        route = jnp.sum(hidden * proj, axis=1, keepdims=True)
        scaled = weights * proj
        d_gate = (scaled * up * sig * (1.0 + gate * (1.0 - sig))).astype(BF16)
        d_up = (scaled * gate * sig).astype(BF16)
        dgu[pl.ds(base, ROWS), 0:HID] = d_gate
        dgu[pl.ds(base, ROWS), HID : 2 * HID] = d_up
        wtd[pl.ds(base, ROWS), :] = (weights * hidden).astype(BF16)
        lane = lax.broadcasted_iota(jnp.int32, (SRC, LANES), 1)
        line = jnp.zeros((SRC, LANES), F32)
        for j in range(CAP):
            line = line + jnp.where(lane == j, route[j * SRC : (j + 1) * SRC, :], 0.0)
        retf[pl.ds(CAP * COLS, SRC, stride=RPITCH), :] = line

        def spread(m, carry):
            cols = pl.ds(pl.multiple_of(m * 512, 512), 512)
            piece = jnp.dot(dgu[pl.ds(base, ROWS), :], wgut[:, cols], preferred_element_type=F32)
            for h in range(4):
                for j in range(CAP):
                    retf[pl.ds(j * COLS + m * 4 + h, SRC, stride=RPITCH), :] = piece[
                        j * SRC : (j + 1) * SRC, h * LANES : (h + 1) * LANES
                    ]
            return carry

        lax.fori_loop(0, FEAT // 512, spread, 0)
        for ref, core in ((pst, 1 - c), (own, c)):
            for i in range(2 * STEP):
                ref[g, i * RROWS : (i + 1) * RROWS, :] = retf[
                    pl.ds((core * (2 * STEP) + i) * RPITCH, RROWS), :
                ].astype(BF16)
            if ref is pst:
                part(g).start()

    def reply(g):
        part(g).wait_recv()
        rsend[g] = (own[g].astype(F32) + prt[g].astype(F32)).astype(BF16)

    def local(g):
        return pltpu.make_async_copy(
            rsend.at[0, pl.ds(pl.multiple_of(xl * RROWS, 16), RROWS)], ret.at[0, xl * STEP], ret_sem.at[0]
        )

    def grads(low, high, first, last):
        tn = (((0,), (0,)), ((), ()))

        def tile(m, carry):
            at = pl.ds(pl.multiple_of(m * 512, 512), 512)
            far = pl.ds(pl.multiple_of(FEAT + m * 512, 512), 512)
            both = lax.dot_general(rows[low:high, at], dgu[low:high, :], tn, preferred_element_type=F32)
            down = lax.dot_general(wtd[low:high, :], rows[low:high, far], tn, preferred_element_type=F32)
            gate, up = both[:, 0:HID], both[:, HID : 2 * HID]
            if low > 0:
                gate, up = gate + sg[at, :].astype(F32), up + su[at, :].astype(F32)
                down = down + sd[:, at].astype(F32)
            sg[at, :] = gate.astype(BF16)
            su[at, :] = up.astype(BF16)
            sd[:, at] = down.astype(BF16)
            return carry

        lax.fori_loop(first, last, tile, 0)

    def chunk(g, carry):
        take(g)

        @pl.when(g == 1)
        def _():
            reply(0)
            local(0).start()
            back(0, 0, 1 - xl).start()
            for i in range(2, 2 * STEP):
                back(0, i, i % 2).start()

        @pl.when(g > 1)
        def _():
            reply(g - 1)
            for i in range(2 * STEP):
                back(g - 1, i, i % 2).start()

        @pl.when(g >= 4)
        def _():
            grads(0, SPAN, (g - 4) * 2, jnp.minimum((g - 4) * 2 + 2, FEAT // 512))

        forward(g).wait_recv()
        compute(g)
        return carry

    lax.fori_loop(0, CHUNKS, chunk, 0)
    reply(CHUNKS - 1)
    for i in range(2 * STEP):
        back(CHUNKS - 1, i, i % 2).start()

    grads(SPAN, ALL, 0, FEAT // 512)

    def collect(g, carry):
        pltpu.make_async_copy(ret.at[g], ret.at[g], ret_sem.at[g]).wait()
        for xs in range(2):
            for kq in range(STEP):
                at = (xs * EXP + g * STEP + kq) * RPITCH
                flat[pl.ds(at, RROWS), :] = ret[g, xs * STEP + kq].astype(F32)
        return carry

    lax.fori_loop(0, CHUNKS, collect, 0)

    remote(0, 1 - xl).wait_send()
    back(0, 0, 1 - xl).wait_send()

    def drain(k, carry):
        remote(k, 0).wait_send()
        remote(k, 1).wait_send()
        return carry

    lax.fori_loop(1, EXP, drain, 0)

    def drain_back(i, carry):
        pltpu.make_async_copy(
            rsend.at[0, pl.ds(0, RROWS)], rsend.at[0, pl.ds(0, RROWS)], rs_sem.at[i]
        ).wait()
        return carry

    lax.fori_loop(2, CHUNKS * 2 * STEP, drain_back, 0)

    def drain_pairs(g, carry):
        forward(g).wait_send()
        part(g).wait_send()
        return carry

    lax.fori_loop(0, CHUNKS, drain_pairs, 0)


def finish(
    ids_ref, flat, slots, sg, su, sd, gt_hbm, gr_hbm, gg_hbm, gu_hbm, gd_hbm, got, gtv, grv, sem
):
    pairs = ((sg, gg_hbm), (su, gu_hbm), (sd, gd_hbm), (gtv, gt_hbm), (grv, gr_hbm))
    copies = [pltpu.make_async_copy(v, h, sem.at[i]) for i, (v, h) in enumerate(pairs)]
    for copy in copies[:3]:
        copy.start()
    target = targets(lax.axis_index("expert"))
    tn = (((0,), (0,)), ((), ()))

    def merge(q, carry):
        for h in range(2):
            col = q * 2 + h
            for j in range(CAP):
                near = flat[pl.ds(j * COLS + col, EXP, stride=RPITCH), :]
                far = flat[pl.ds(EXP * RPITCH + j * COLS + col, EXP, stride=RPITCH), :]
                got[j * EXP : (j + 1) * EXP, pl.ds(pl.multiple_of(col * LANES, LANES), LANES)] = (
                    near + far
                ).astype(BF16)
        return carry

    lax.fori_loop(0, COLS // 2, merge, 0)
    line = (
        flat[pl.ds(CAP * COLS, EXP, stride=RPITCH), :]
        + flat[pl.ds(EXP * RPITCH + CAP * COLS, EXP, stride=RPITCH), :]
    )
    spot = jnp.zeros((EXP, TOK), F32)
    for j in range(CAP):
        spot = spot + slots[j * EXP : (j + 1) * EXP, :].astype(F32) * line[:, j : j + 1]
    for q in range(8):
        grv[q : q + 1, :] = jnp.sum(
            jnp.where(ids_ref[q : q + 1, :] == target, spot, 0.0), axis=0, keepdims=True
        ).astype(BF16)

    def place(m, carry):
        at = pl.ds(pl.multiple_of(m * 512, 512), 512)
        gtv[:, at] = lax.dot_general(slots[...], got[:, at], tn, preferred_element_type=F32).astype(BF16)
        return carry

    lax.fori_loop(0, FEAT // 512, place, 0)
    for copy in copies[3:]:
        copy.start()
    for copy in copies:
        copy.wait()


def shards(tokens, out_grad, expert_ids, route_weights, w_gate, w_up, w_down):
    vmem = pl.BlockSpec(memory_space=pltpu.VMEM)
    anywhere = pl.BlockSpec(memory_space=pl.ANY)
    size = 2 * STEP * RROWS
    dma = pltpu.SemaphoreType.DMA
    shapes = ((TOK, FEAT), (8, TOK), (FEAT, HID), (FEAT, HID), (HID, FEAT))
    kept = (((2 * EXP * RPITCH, LANES), F32), ((CAP * EXP, TOK), BF16)) + tuple((s, BF16) for s in shapes[2:])
    made = pl.pallas_call(
        body,
        out_shape=tuple(pltpu.VMEM(s, t) for s, t in kept),
        in_specs=[vmem, vmem, vmem, vmem, anywhere, anywhere, anywhere],
        out_specs=(vmem,) * 5,
        scratch_shapes=[
            pltpu.VMEM((FEAT, 2 * HID), BF16),
            pltpu.VMEM((2 * HID, FEAT), BF16),
            pltpu.VMEM((HID, FEAT), BF16),
            pltpu.VMEM((EXP, FROWS, LANES), BF16),
            pltpu.VMEM((CHUNKS, SRC, FROWS, LANES), BF16),
            pltpu.VMEM((ALL, 2 * FEAT), BF16),
            pltpu.VMEM((ALL, 2 * HID), BF16),
            pltpu.VMEM((ALL, HID), BF16),
            pltpu.VMEM((SRC * RPITCH, LANES), F32),
            pltpu.VMEM((CHUNKS, size, LANES), BF16),
            pltpu.VMEM((CHUNKS, size, LANES), BF16),
            pltpu.VMEM((CHUNKS, size, LANES), BF16),
            pltpu.VMEM((CHUNKS, size, LANES), BF16),
            pltpu.VMEM((CHUNKS, 2 * STEP, RROWS, LANES), BF16),
            pltpu.VMEM((EXP // 8, CAP * 8, TOK), F32),
            dma((2 * EXP,)),
            dma((CHUNKS,)),
            dma((CHUNKS,)),
            dma((CHUNKS,)),
            dma((CHUNKS,)),
            dma((CHUNKS,)),
            dma((2 * EXP,)),
            dma((CHUNKS,)),
            dma((3,)),
        ],
        compiler_params=pltpu.CompilerParams(
            collective_id=0, has_side_effects=True, vmem_limit_bytes=52_000_000
        ),
    )(
        expert_ids.T,
        route_weights.T,
        tokens,
        out_grad,
        w_gate[0],
        w_up[0],
        w_down[0],
    )
    made = [pltpu.with_memory_space_constraint(m, pltpu.VMEM) for m in made]
    grad_tokens, grad_route, grad_g, grad_u, grad_d = pl.pallas_call(
        finish,
        out_shape=tuple(jax.ShapeDtypeStruct(s, BF16) for s in shapes),
        in_specs=[vmem] * 6,
        out_specs=(anywhere,) * 5,
        scratch_shapes=[
            pltpu.VMEM((CAP * EXP, FEAT), BF16),
            pltpu.VMEM((TOK, FEAT), BF16),
            pltpu.VMEM((8, TOK), BF16),
            dma((5,)),
        ],
        compiler_params=pltpu.CompilerParams(vmem_limit_bytes=16_000_000),
    )(expert_ids.T, *made)
    return (grad_tokens, grad_route.T, grad_g[None], grad_u[None], grad_d[None])


def solution(mesh):
    rows_spec = P(("expert", "dp"), None)
    hidden_last = P("expert", None, "dp")
    hidden_mid = P("expert", "dp", None)
    return jax.shard_map(
        shards,
        mesh=mesh,
        in_specs=(rows_spec,) * 4 + (hidden_last, hidden_last, hidden_mid),
        out_specs=(rows_spec, rows_spec, hidden_last, hidden_last, hidden_mid),
        check_vma=False,
    )
```

```python
import jax
import jax.numpy as jnp
from jax import lax
from jax.experimental import pallas as pl
from jax.experimental.pallas import tpu as pltpu
from jax.sharding import PartitionSpec as P

NZ, NY, NX = 4, 4, 2
EXP = NZ * NY * NX
CAP = 5
STEP = 4
CHUNKS = EXP // STEP
LANES = 128
FEAT = 3584
HID = 256
COLS = FEAT // LANES
FROWS = 288
RROWS = 144
FPITCH, RPITCH = FROWS + 1, RROWS + 1
SRC = 4 * STEP
ROWS = SRC * CAP
ALL = ROWS * CHUNKS
TOK = 128
MESH = pl.DeviceIdType.MESH
F32, BF16 = jnp.float32, jnp.bfloat16


def steps(k):
    kz = k & 3
    return kz, (kz + (k >> 2)) & 3, (kz + (k >> 4)) & 1


def shifted(e, k, sign):
    z, y, x = e >> 3, (e >> 1) & 3, e & 1
    kz, ky, kx = steps(k)
    z = (z + NZ + sign * kz) & 3
    y = (y + NY + sign * ky) & 3
    x = (x + NX + sign * kx) & 1
    return (z << 3) + (y << 1) + x


def targets(e):
    z, y, x = e >> 3, (e >> 1) & 3, e & 1
    kz, ky, kx = steps(lax.broadcasted_iota(jnp.int32, (EXP, TOK), 0))
    return (((z + kz) & 3) << 3) + (((y + ky) & 3) << 1) + ((x + kx) & 1)


def body(
    ids_ref, rw_ref, tok_hbm, dy_hbm, wg_hbm, wu_hbm, wd_hbm,
    flat, slots, sg, su, sd,
    wgu, wgut, wd, send, recv, rows, dgu, wtd, retf, own, pst, prt, rsend, ret, early, tok_ref, dy_ref,
    send_sem, recv_sem, fws_sem, fwr_sem, pas_sem, par_sem, rs_sem, ret_sem, win_sem, row_sem,
):
    e = lax.axis_index("expert")
    d = lax.axis_index("dp")
    xl, c = d >> 1, d & 1
    partner = {"expert": e, "dp": xl * 2 + 1 - c}

    fetch = [
        pltpu.make_async_copy(h, v, row_sem.at[i])
        for i, (h, v) in enumerate(((tok_hbm, tok_ref), (dy_hbm, dy_ref)))
    ]
    for copy in fetch:
        copy.start()

    barrier = pltpu.get_barrier_semaphore()

    def greet(k, xd):
        there = {"expert": shifted(e, k, 1), "dp": xd * 2 + c}
        pl.semaphore_signal(barrier, inc=1, device_id=there, device_id_type=MESH)

    def greet_both(k, carry):
        greet(k, 0)
        greet(k, 1)
        return carry

    greet(0, 1 - xl)
    pl.semaphore_signal(barrier, inc=1, device_id=partner, device_id_type=MESH)
    lax.fori_loop(1, EXP, greet_both, 0)

    loads = [
        pltpu.make_async_copy(h, v, win_sem.at[i])
        for i, (h, v) in enumerate(((wg_hbm, wgu.at[:, 0:HID]), (wu_hbm, wgu.at[:, HID : 2 * HID]), (wd_hbm, wd)))
    ]
    for copy in loads:
        copy.start()

    target = targets(e)
    chosen = jnp.zeros((EXP, TOK), F32)
    weight = jnp.zeros((EXP, TOK), F32)
    rw = rw_ref[...].astype(F32)
    for q in range(8):
        same = ids_ref[q : q + 1, :] == target
        chosen = chosen + jnp.where(same, 1.0, 0.0)
        weight = weight + jnp.where(same, rw[q : q + 1, :], 0.0)
    before = lax.broadcasted_iota(jnp.int32, (TOK, TOK), 0) < lax.broadcasted_iota(
        jnp.int32, (TOK, TOK), 1
    )
    rank = jnp.dot(
        chosen.astype(BF16), jnp.where(before, 1.0, 0.0).astype(BF16), preferred_element_type=F32
    )
    for j in range(CAP):
        hot = jnp.where(jnp.abs(rank - j) < 0.5, chosen, 0.0)
        slots[j * EXP : (j + 1) * EXP, :] = hot.astype(BF16)
        for p in range(EXP // 8):
            early[p, j * 8 : (j + 1) * 8, :] = hot[p * 8 : (p + 1) * 8, :]
        one = jnp.sum(hot * weight, axis=1, keepdims=True)
        flat[pl.ds(2 * CAP * COLS + j, EXP, stride=FPITCH), :] = jnp.broadcast_to(one, (EXP, LANES))
    for j in range(2 * CAP * COLS + CAP, FROWS):
        flat[pl.ds(j, EXP, stride=FPITCH), :] = jnp.zeros((EXP, LANES), F32)
    for j in range(CAP * COLS + 1, RROWS):
        retf[pl.ds(j, SRC, stride=RPITCH), :] = jnp.zeros((SRC, LANES), F32)

    def remote(k, xd):
        g, kq = k >> 2, k & 3
        return pltpu.make_async_remote_copy(
            src_ref=send.at[k],
            dst_ref=recv.at[g, c * (2 * STEP) + kq * 2 + xl],
            send_sem=send_sem.at[k * 2 + xd],
            recv_sem=recv_sem.at[g],
            device_id={"expert": shifted(e, k, 1), "dp": xd * 2 + c},
            device_id_type=MESH,
        )

    def pack(k):
        send[k] = flat[pl.ds(k * FPITCH, FROWS), :].astype(BF16)

    def issue(k, carry):
        pack(k)
        remote(k, 0).start()
        remote(k, 1).start()
        return carry

    def pick(p):
        hots = early[p].astype(BF16)

        def gather(m, carry):
            for a, ref in enumerate((tok_ref, dy_ref)):
                picked = jnp.dot(
                    hots, ref[:, pl.ds(pl.multiple_of(m * 512, 512), 512)], preferred_element_type=F32
                )
                for h in range(4):
                    for j in range(CAP):
                        at = p * 8 * FPITCH + j * 2 * COLS + a * COLS + m * 4 + h
                        flat[pl.ds(at, 8, stride=FPITCH), :] = picked[
                            j * 8 : (j + 1) * 8, h * LANES : (h + 1) * LANES
                        ]
            return carry

        lax.fori_loop(0, FEAT // 512, gather, 0)

    for copy in fetch:
        copy.wait()
    pick(0)
    pack(0)
    pl.semaphore_wait(barrier, 2 * EXP)
    remote(0, 1 - xl).start()
    pltpu.make_async_copy(send.at[0], recv.at[0, c * (2 * STEP) + xl], recv_sem.at[0]).start()
    lax.fori_loop(1, 8, issue, 0)

    def later(p, carry):
        pick(p)
        lax.fori_loop(p * 8, p * 8 + 8, issue, 0)
        return carry

    lax.fori_loop(1, EXP // 8, later, 0)
    for copy in loads:
        copy.wait()

    def turn(m, carry):
        at = pl.ds(pl.multiple_of(m * 512, 512), 512)
        wgut[:, at] = wgu[at, :].T
        return carry

    lax.fori_loop(0, FEAT // 512, turn, 0)

    def half(g, core):
        return recv.at[g, pl.ds(core * (2 * STEP), 2 * STEP)]

    def forward(g):
        return pltpu.make_async_remote_copy(
            src_ref=half(g, c), dst_ref=half(g, c), send_sem=fws_sem.at[g], recv_sem=fwr_sem.at[g],
            device_id=partner, device_id_type=MESH,
        )

    def take(g):
        pltpu.make_async_copy(half(g, c), half(g, c), recv_sem.at[g]).wait()
        forward(g).start()

    def part(g):
        return pltpu.make_async_remote_copy(
            src_ref=pst.at[g], dst_ref=prt.at[g], send_sem=pas_sem.at[g], recv_sem=par_sem.at[g],
            device_id=partner, device_id_type=MESH,
        )

    def back(g, i, xs):
        kq = i // 2
        return pltpu.make_async_remote_copy(
            src_ref=rsend.at[g, pl.ds(pl.multiple_of((kq * 2 + xs) * RROWS, 16), RROWS)],
            dst_ref=ret.at[g, xl * STEP + kq],
            send_sem=rs_sem.at[g * (2 * STEP) + i],
            recv_sem=ret_sem.at[g],
            device_id={"expert": shifted(e, g * STEP + kq, -1), "dp": xs * 2 + c},
            device_id_type=MESH,
        )

    def compute(g):
        def widen(s, carry):
            flat[pl.ds(s * FPITCH, FROWS), :] = recv[g, s].astype(F32)
            return carry

        lax.fori_loop(0, SRC, widen, 0)
        base = pl.multiple_of(g * ROWS, 16)

        def order(q, carry):
            for h in range(4):
                col = q * 4 + h
                for j in range(CAP):
                    piece = flat[pl.ds(j * 2 * COLS + col, SRC, stride=FPITCH), :]
                    rows[
                        pl.ds(pl.multiple_of(base + j * SRC, 16), SRC),
                        pl.ds(pl.multiple_of(col * LANES, LANES), LANES),
                    ] = piece.astype(BF16)
            return carry

        lax.fori_loop(0, 2 * COLS // 4, order, 0)
        weights = jnp.concatenate(
            [flat[pl.ds(2 * CAP * COLS + j, SRC, stride=FPITCH), :] for j in range(CAP)], axis=0
        )
        weights = jnp.concatenate([weights, weights], axis=1)
        xs = rows[pl.ds(base, ROWS), 0:FEAT]
        dys = rows[pl.ds(base, ROWS), FEAT : 2 * FEAT]
        both = jnp.dot(xs, wgu[...], preferred_element_type=F32)
        gate, up = both[:, 0:HID], both[:, HID : 2 * HID]
        proj = lax.dot_general(dys, wd[...], (((1,), (1,)), ((), ())), preferred_element_type=F32)
        sig = jax.nn.sigmoid(gate)
        hidden = (gate * sig * up).astype(BF16).astype(F32)
        route = jnp.sum(hidden * proj, axis=1, keepdims=True)
        scaled = weights * proj
        d_gate = (scaled * up * sig * (1.0 + gate * (1.0 - sig))).astype(BF16)
        d_up = (scaled * gate * sig).astype(BF16)
        dgu[pl.ds(base, ROWS), 0:HID] = d_gate
        dgu[pl.ds(base, ROWS), HID : 2 * HID] = d_up
        wtd[pl.ds(base, ROWS), :] = (weights * hidden).astype(BF16)
        lane = lax.broadcasted_iota(jnp.int32, (SRC, LANES), 1)
        line = jnp.zeros((SRC, LANES), F32)
        for j in range(CAP):
            line = line + jnp.where(lane == j, route[j * SRC : (j + 1) * SRC, :], 0.0)
        retf[pl.ds(CAP * COLS, SRC, stride=RPITCH), :] = line

        def spread(m, carry):
            cols = pl.ds(pl.multiple_of(m * 512, 512), 512)
            piece = jnp.dot(dgu[pl.ds(base, ROWS), :], wgut[:, cols], preferred_element_type=F32)
            for h in range(4):
                for j in range(CAP):
                    retf[pl.ds(j * COLS + m * 4 + h, SRC, stride=RPITCH), :] = piece[
                        j * SRC : (j + 1) * SRC, h * LANES : (h + 1) * LANES
                    ]
            return carry

        lax.fori_loop(0, FEAT // 512, spread, 0)
        for ref, core in ((pst, 1 - c), (own, c)):
            for i in range(2 * STEP):
                ref[g, i * RROWS : (i + 1) * RROWS, :] = retf[
                    pl.ds((core * (2 * STEP) + i) * RPITCH, RROWS), :
                ].astype(BF16)
            if ref is pst:
                part(g).start()

    def reply(g):
        part(g).wait_recv()
        rsend[g] = (own[g].astype(F32) + prt[g].astype(F32)).astype(BF16)

    def local(g):
        return pltpu.make_async_copy(
            rsend.at[0, pl.ds(pl.multiple_of(xl * RROWS, 16), RROWS)], ret.at[0, xl * STEP], ret_sem.at[0]
        )

    def grads():
        tn = (((0,), (0,)), ((), ()))

        def tile(m, carry):
            at = pl.ds(pl.multiple_of(m * 512, 512), 512)
            far = pl.ds(pl.multiple_of(FEAT + m * 512, 512), 512)
            both = lax.dot_general(rows[:, at], dgu[:, :], tn, preferred_element_type=F32)
            down = lax.dot_general(wtd[:, :], rows[:, far], tn, preferred_element_type=F32)
            gate, up = both[:, 0:HID], both[:, HID : 2 * HID]
            sg[at, :] = gate.astype(BF16)
            su[at, :] = up.astype(BF16)
            sd[:, at] = down.astype(BF16)
            return carry

        lax.fori_loop(0, FEAT // 512, tile, 0)

    def chunk(g, carry):
        take(g)

        @pl.when(g == 1)
        def _():
            reply(0)
            local(0).start()
            back(0, 0, 1 - xl).start()
            for i in range(2, 2 * STEP):
                back(0, i, i % 2).start()

        @pl.when(g > 1)
        def _():
            reply(g - 1)
            for i in range(2 * STEP):
                back(g - 1, i, i % 2).start()

        forward(g).wait_recv()
        compute(g)
        return carry

    lax.fori_loop(0, CHUNKS, chunk, 0)
    reply(CHUNKS - 1)
    for i in range(2 * STEP):
        back(CHUNKS - 1, i, i % 2).start()

    grads()

    def collect(g, carry):
        pltpu.make_async_copy(ret.at[g], ret.at[g], ret_sem.at[g]).wait()
        for xs in range(2):
            for kq in range(STEP):
                at = (xs * EXP + g * STEP + kq) * RPITCH
                flat[pl.ds(at, RROWS), :] = ret[g, xs * STEP + kq].astype(F32)
        return carry

    lax.fori_loop(0, CHUNKS, collect, 0)

    remote(0, 1 - xl).wait_send()
    back(0, 0, 1 - xl).wait_send()

    def drain(k, carry):
        remote(k, 0).wait_send()
        remote(k, 1).wait_send()
        return carry

    lax.fori_loop(1, EXP, drain, 0)

    def drain_back(i, carry):
        pltpu.make_async_copy(
            rsend.at[0, pl.ds(0, RROWS)], rsend.at[0, pl.ds(0, RROWS)], rs_sem.at[i]
        ).wait()
        return carry

    lax.fori_loop(2, CHUNKS * 2 * STEP, drain_back, 0)

    def drain_pairs(g, carry):
        forward(g).wait_send()
        part(g).wait_send()
        return carry

    lax.fori_loop(0, CHUNKS, drain_pairs, 0)


def finish(
    ids_ref, flat, slots, sg, su, sd, gt_hbm, gr_hbm, gg_hbm, gu_hbm, gd_hbm, got, gtv, grv, sem
):
    pairs = ((sg, gg_hbm), (su, gu_hbm), (sd, gd_hbm), (gtv, gt_hbm), (grv, gr_hbm))
    copies = [pltpu.make_async_copy(v, h, sem.at[i]) for i, (v, h) in enumerate(pairs)]
    for copy in copies[:3]:
        copy.start()
    target = targets(lax.axis_index("expert"))
    tn = (((0,), (0,)), ((), ()))

    def merge(q, carry):
        for h in range(2):
            col = q * 2 + h
            for j in range(CAP):
                near = flat[pl.ds(j * COLS + col, EXP, stride=RPITCH), :]
                far = flat[pl.ds(EXP * RPITCH + j * COLS + col, EXP, stride=RPITCH), :]
                got[j * EXP : (j + 1) * EXP, pl.ds(pl.multiple_of(col * LANES, LANES), LANES)] = (
                    near + far
                ).astype(BF16)
        return carry

    lax.fori_loop(0, COLS // 2, merge, 0)
    line = (
        flat[pl.ds(CAP * COLS, EXP, stride=RPITCH), :]
        + flat[pl.ds(EXP * RPITCH + CAP * COLS, EXP, stride=RPITCH), :]
    )
    spot = jnp.zeros((EXP, TOK), F32)
    for j in range(CAP):
        spot = spot + slots[j * EXP : (j + 1) * EXP, :].astype(F32) * line[:, j : j + 1]
    for q in range(8):
        grv[q : q + 1, :] = jnp.sum(
            jnp.where(ids_ref[q : q + 1, :] == target, spot, 0.0), axis=0, keepdims=True
        ).astype(BF16)

    def place(m, carry):
        at = pl.ds(pl.multiple_of(m * 512, 512), 512)
        gtv[:, at] = lax.dot_general(slots[...], got[:, at], tn, preferred_element_type=F32).astype(BF16)
        return carry

    lax.fori_loop(0, FEAT // 512, place, 0)
    for copy in copies[3:]:
        copy.start()
    for copy in copies:
        copy.wait()


def shards(tokens, out_grad, expert_ids, route_weights, w_gate, w_up, w_down):
    vmem = pl.BlockSpec(memory_space=pltpu.VMEM)
    anywhere = pl.BlockSpec(memory_space=pl.ANY)
    size = 2 * STEP * RROWS
    dma = pltpu.SemaphoreType.DMA
    shapes = ((TOK, FEAT), (8, TOK), (FEAT, HID), (FEAT, HID), (HID, FEAT))
    kept = (((2 * EXP * RPITCH, LANES), F32), ((CAP * EXP, TOK), BF16)) + tuple((s, BF16) for s in shapes[2:])
    made = pl.pallas_call(
        body,
        out_shape=tuple(pltpu.VMEM(s, t) for s, t in kept),
        in_specs=[vmem, vmem] + [anywhere] * 5,
        out_specs=(vmem,) * 5,
        scratch_shapes=[
            pltpu.VMEM((FEAT, 2 * HID), BF16),
            pltpu.VMEM((2 * HID, FEAT), BF16),
            pltpu.VMEM((HID, FEAT), BF16),
            pltpu.VMEM((EXP, FROWS, LANES), BF16),
            pltpu.VMEM((CHUNKS, SRC, FROWS, LANES), BF16),
            pltpu.VMEM((ALL, 2 * FEAT), BF16),
            pltpu.VMEM((ALL, 2 * HID), BF16),
            pltpu.VMEM((ALL, HID), BF16),
            pltpu.VMEM((SRC * RPITCH, LANES), F32),
            pltpu.VMEM((CHUNKS, size, LANES), BF16),
            pltpu.VMEM((CHUNKS, size, LANES), BF16),
            pltpu.VMEM((CHUNKS, size, LANES), BF16),
            pltpu.VMEM((CHUNKS, size, LANES), BF16),
            pltpu.VMEM((CHUNKS, 2 * STEP, RROWS, LANES), BF16),
            pltpu.VMEM((EXP // 8, CAP * 8, TOK), F32),
            pltpu.VMEM((TOK, FEAT), BF16),
            pltpu.VMEM((TOK, FEAT), BF16),
            dma((2 * EXP,)),
            dma((CHUNKS,)),
            dma((CHUNKS,)),
            dma((CHUNKS,)),
            dma((CHUNKS,)),
            dma((CHUNKS,)),
            dma((2 * EXP,)),
            dma((CHUNKS,)),
            dma((3,)),
            dma((2,)),
        ],
        compiler_params=pltpu.CompilerParams(
            collective_id=0, has_side_effects=True, vmem_limit_bytes=52_000_000
        ),
    )(
        expert_ids.T,
        route_weights.T,
        tokens,
        out_grad,
        w_gate[0],
        w_up[0],
        w_down[0],
    )
    made = [pltpu.with_memory_space_constraint(m, pltpu.VMEM) for m in made]
    grad_tokens, grad_route, grad_g, grad_u, grad_d = pl.pallas_call(
        finish,
        out_shape=tuple(jax.ShapeDtypeStruct(s, BF16) for s in shapes),
        in_specs=[vmem] * 6,
        out_specs=(anywhere,) * 5,
        scratch_shapes=[
            pltpu.VMEM((CAP * EXP, FEAT), BF16),
            pltpu.VMEM((TOK, FEAT), BF16),
            pltpu.VMEM((8, TOK), BF16),
            dma((5,)),
        ],
        compiler_params=pltpu.CompilerParams(vmem_limit_bytes=16_000_000),
    )(expert_ids.T, *made)
    return (grad_tokens, grad_route.T, grad_g[None], grad_u[None], grad_d[None])


def solution(mesh):
    rows_spec = P(("expert", "dp"), None)
    hidden_last = P("expert", None, "dp")
    hidden_mid = P("expert", "dp", None)
    return jax.shard_map(
        shards,
        mesh=mesh,
        in_specs=(rows_spec,) * 4 + (hidden_last, hidden_last, hidden_mid),
        out_specs=(rows_spec, rows_spec, hidden_last, hidden_last, hidden_mid),
        check_vma=False,
    )
```

```python
import jax
import jax.numpy as jnp
from jax import lax
from jax.experimental import pallas as pl
from jax.experimental.pallas import tpu as pltpu
from jax.sharding import PartitionSpec as P

NZ, NY, NX = 4, 4, 2
EXP = NZ * NY * NX
CAP = 5
STEP = 4
CHUNKS = EXP // STEP
LANES = 128
FEAT = 3584
HID = 256
COLS = FEAT // LANES
FROWS = 288
RROWS = 144
FPITCH, RPITCH = FROWS + 1, RROWS + 1
SPARE = 320
SRC = 4 * STEP
ROWS = SRC * CAP
ALL = ROWS * CHUNKS
TOK = 128
MESH = pl.DeviceIdType.MESH
F32, BF16 = jnp.float32, jnp.bfloat16


def steps(k):
    kz = k & 3
    return kz, (kz + (k >> 2)) & 3, (kz + (k >> 4)) & 1


def shifted(e, k, sign):
    z, y, x = e >> 3, (e >> 1) & 3, e & 1
    kz, ky, kx = steps(k)
    z = (z + NZ + sign * kz) & 3
    y = (y + NY + sign * ky) & 3
    x = (x + NX + sign * kx) & 1
    return (z << 3) + (y << 1) + x


def targets(e):
    z, y, x = e >> 3, (e >> 1) & 3, e & 1
    kz, ky, kx = steps(lax.broadcasted_iota(jnp.int32, (EXP, TOK), 0))
    return (((z + kz) & 3) << 3) + (((y + ky) & 3) << 1) + ((x + kx) & 1)


def body(
    ids_ref, rw_ref, tok_hbm, dy_hbm, wg_hbm, wu_hbm, wd_hbm,
    flat, slots, sg, su, sd,
    wgu, wgut, wd, send, recv, rows, dgu, wtd, retf, own, pst, prt, rsend, ret, early, tok_ref, dy_ref,
    send_sem, recv_sem, fws_sem, fwr_sem, pas_sem, par_sem, rs_sem, ret_sem, win_sem, row_sem,
):
    e = lax.axis_index("expert")
    d = lax.axis_index("dp")
    xl, c = d >> 1, d & 1
    partner = {"expert": e, "dp": xl * 2 + 1 - c}

    fetch = [
        pltpu.make_async_copy(h, v, row_sem.at[i])
        for i, (h, v) in enumerate(((tok_hbm, tok_ref), (dy_hbm, dy_ref)))
    ]
    for copy in fetch:
        copy.start()

    barrier = pltpu.get_barrier_semaphore()

    def greet(k, xd):
        there = {"expert": shifted(e, k, 1), "dp": xd * 2 + c}
        pl.semaphore_signal(barrier, inc=1, device_id=there, device_id_type=MESH)

    def greet_both(k, carry):
        greet(k, 0)
        greet(k, 1)
        return carry

    greet(0, 1 - xl)
    pl.semaphore_signal(barrier, inc=1, device_id=partner, device_id_type=MESH)
    lax.fori_loop(1, EXP, greet_both, 0)

    loads = [
        pltpu.make_async_copy(h, v, win_sem.at[i])
        for i, (h, v) in enumerate(((wg_hbm, wgu.at[:, 0:HID]), (wu_hbm, wgu.at[:, HID : 2 * HID]), (wd_hbm, wd)))
    ]
    for copy in loads:
        copy.start()

    target = targets(e)
    chosen = jnp.zeros((EXP, TOK), F32)
    weight = jnp.zeros((EXP, TOK), F32)
    rw = rw_ref[...].astype(F32)
    for q in range(8):
        same = ids_ref[q : q + 1, :] == target
        chosen = chosen + jnp.where(same, 1.0, 0.0)
        weight = weight + jnp.where(same, rw[q : q + 1, :], 0.0)
    before = lax.broadcasted_iota(jnp.int32, (TOK, TOK), 0) < lax.broadcasted_iota(
        jnp.int32, (TOK, TOK), 1
    )
    rank = jnp.dot(
        chosen.astype(BF16), jnp.where(before, 1.0, 0.0).astype(BF16), preferred_element_type=F32
    )
    for j in range(CAP):
        hot = jnp.where(jnp.abs(rank - j) < 0.5, chosen, 0.0)
        slots[j * EXP : (j + 1) * EXP, :] = hot.astype(BF16)
        for p in range(EXP // 8):
            early[p, j * 8 : (j + 1) * 8, :] = hot[p * 8 : (p + 1) * 8, :]
        one = jnp.sum(hot * weight, axis=1, keepdims=True)
        flat[pl.ds(2 * CAP * COLS + j, EXP, stride=FPITCH), :] = jnp.broadcast_to(one, (EXP, LANES))
    for j in range(2 * CAP * COLS + CAP, FROWS):
        flat[pl.ds(j, EXP, stride=FPITCH), :] = jnp.zeros((EXP, LANES), F32)
    for j in range(CAP * COLS + 1, RROWS):
        retf[pl.ds(j, SRC, stride=RPITCH), :] = jnp.zeros((SRC, LANES), F32)

    def remote(k, xd):
        g, kq = k >> 2, k & 3
        return pltpu.make_async_remote_copy(
            src_ref=send.at[k],
            dst_ref=recv.at[g, c * (2 * STEP) + kq * 2 + xl],
            send_sem=send_sem.at[k * 2 + xd],
            recv_sem=recv_sem.at[g],
            device_id={"expert": shifted(e, k, 1), "dp": xd * 2 + c},
            device_id_type=MESH,
        )

    def pack(k):
        send[k] = flat[pl.ds(k * FPITCH, FROWS), :].astype(BF16)

    def issue(k, carry):
        pack(k)
        remote(k, 0).start()
        remote(k, 1).start()
        return carry

    def pick(p):
        hots = early[p].astype(BF16)

        def gather(m, carry):
            for a, ref in enumerate((tok_ref, dy_ref)):
                picked = jnp.dot(
                    hots, ref[:, pl.ds(pl.multiple_of(m * 512, 512), 512)], preferred_element_type=F32
                )
                for h in range(4):
                    for j in range(CAP):
                        at = p * 8 * FPITCH + j * 2 * COLS + a * COLS + m * 4 + h
                        flat[pl.ds(at, 8, stride=FPITCH), :] = picked[
                            j * 8 : (j + 1) * 8, h * LANES : (h + 1) * LANES
                        ]
            return carry

        lax.fori_loop(0, FEAT // 512, gather, 0)

    for copy in fetch:
        copy.wait()
    pick(0)
    pack(0)
    pl.semaphore_wait(barrier, 2 * EXP)
    remote(0, 1 - xl).start()
    pltpu.make_async_copy(send.at[0], recv.at[0, c * (2 * STEP) + xl], recv_sem.at[0]).start()
    lax.fori_loop(1, 8, issue, 0)

    def later(p, carry):
        pick(p)
        lax.fori_loop(p * 8, p * 8 + 8, issue, 0)
        return carry

    lax.fori_loop(1, EXP // 8, later, 0)
    for copy in loads:
        copy.wait()

    def turn(m, carry):
        at = pl.ds(pl.multiple_of(m * 512, 512), 512)
        wgut[:, at] = wgu[at, :].T
        return carry

    lax.fori_loop(0, FEAT // 512, turn, 0)

    def half(g, core):
        return recv.at[g, pl.ds(core * (2 * STEP), 2 * STEP)]

    def forward(g):
        return pltpu.make_async_remote_copy(
            src_ref=half(g, c), dst_ref=half(g, c), send_sem=fws_sem.at[g], recv_sem=fwr_sem.at[g],
            device_id=partner, device_id_type=MESH,
        )

    def take(g):
        pltpu.make_async_copy(half(g, c), half(g, c), recv_sem.at[g]).wait()
        forward(g).start()

    def part(g):
        return pltpu.make_async_remote_copy(
            src_ref=pst.at[g], dst_ref=prt.at[g], send_sem=pas_sem.at[g], recv_sem=par_sem.at[g],
            device_id=partner, device_id_type=MESH,
        )

    def back(g, i, xs):
        kq = i // 2
        return pltpu.make_async_remote_copy(
            src_ref=rsend.at[g, pl.ds(pl.multiple_of((kq * 2 + xs) * RROWS, 16), RROWS)],
            dst_ref=ret.at[g, xl * STEP + kq],
            send_sem=rs_sem.at[g * (2 * STEP) + i],
            recv_sem=ret_sem.at[g],
            device_id={"expert": shifted(e, g * STEP + kq, -1), "dp": xs * 2 + c},
            device_id_type=MESH,
        )

    def compute(g):
        def widen(s, carry):
            flat[pl.ds(s * FPITCH, FROWS), :] = recv[g, s].astype(F32)
            return carry

        lax.fori_loop(0, SRC, widen, 0)
        base = pl.multiple_of(g * ROWS, 16)

        def order(q, carry):
            for h in range(4):
                col = q * 4 + h
                for j in range(CAP):
                    piece = flat[pl.ds(j * 2 * COLS + col, SRC, stride=FPITCH), :]
                    rows[
                        pl.ds(pl.multiple_of(base + j * SRC, 16), SRC),
                        pl.ds(pl.multiple_of(col * LANES, LANES), LANES),
                    ] = piece.astype(BF16)
            return carry

        lax.fori_loop(0, 2 * COLS // 4, order, 0)
        weights = jnp.concatenate(
            [flat[pl.ds(2 * CAP * COLS + j, SRC, stride=FPITCH), :] for j in range(CAP)], axis=0
        )
        weights = jnp.concatenate([weights, weights], axis=1)
        xs = rows[pl.ds(base, ROWS), 0:FEAT]
        dys = rows[pl.ds(base, ROWS), FEAT : 2 * FEAT]
        both = jnp.dot(xs, wgu[...], preferred_element_type=F32)
        gate, up = both[:, 0:HID], both[:, HID : 2 * HID]
        proj = lax.dot_general(dys, wd[...], (((1,), (1,)), ((), ())), preferred_element_type=F32)
        sig = jax.nn.sigmoid(gate)
        hidden = (gate * sig * up).astype(BF16).astype(F32)
        route = jnp.sum(hidden * proj, axis=1, keepdims=True)
        scaled = weights * proj
        d_gate = (scaled * up * sig * (1.0 + gate * (1.0 - sig))).astype(BF16)
        d_up = (scaled * gate * sig).astype(BF16)
        dgu[pl.ds(base, ROWS), 0:HID] = d_gate
        dgu[pl.ds(base, ROWS), HID : 2 * HID] = d_up
        wtd[pl.ds(base, ROWS), :] = (weights * hidden).astype(BF16)
        lane = lax.broadcasted_iota(jnp.int32, (SRC, LANES), 1)
        line = jnp.zeros((SRC, LANES), F32)
        for j in range(CAP):
            line = line + jnp.where(lane == j, route[j * SRC : (j + 1) * SRC, :], 0.0)
        retf[pl.ds(CAP * COLS, SRC, stride=RPITCH), :] = line

        def spread(m, carry):
            cols = pl.ds(pl.multiple_of(m * 512, 512), 512)
            piece = jnp.dot(dgu[pl.ds(base, ROWS), :], wgut[:, cols], preferred_element_type=F32)
            for h in range(4):
                for j in range(CAP):
                    retf[pl.ds(j * COLS + m * 4 + h, SRC, stride=RPITCH), :] = piece[
                        j * SRC : (j + 1) * SRC, h * LANES : (h + 1) * LANES
                    ]
            return carry

        lax.fori_loop(0, FEAT // 512, spread, 0)
        for ref, core in ((pst, 1 - c), (own, c)):
            for i in range(2 * STEP):
                ref[g, i * RROWS : (i + 1) * RROWS, :] = retf[
                    pl.ds((core * (2 * STEP) + i) * RPITCH, RROWS), :
                ].astype(BF16)
            if ref is pst:
                part(g).start()

    def reply(g):
        part(g).wait_recv()
        rsend[g] = (own[g].astype(F32) + prt[g].astype(F32)).astype(BF16)

    def local(g):
        return pltpu.make_async_copy(
            rsend.at[0, pl.ds(pl.multiple_of(xl * RROWS, 16), RROWS)], ret.at[0, xl * STEP], ret_sem.at[0]
        )

    def grads():
        tn = (((0,), (0,)), ((), ()))

        def tile(m, carry):
            at = pl.ds(pl.multiple_of(m * 512, 512), 512)
            far = pl.ds(pl.multiple_of(FEAT + m * 512, 512), 512)
            both = lax.dot_general(rows[:, at], dgu[:, :], tn, preferred_element_type=F32)
            down = lax.dot_general(wtd[:, :], rows[:, far], tn, preferred_element_type=F32)
            gate, up = both[:, 0:HID], both[:, HID : 2 * HID]
            sg[at, :] = gate.astype(BF16)
            su[at, :] = up.astype(BF16)
            sd[:, at] = down.astype(BF16)
            return carry

        lax.fori_loop(0, FEAT // 512, tile, 0)

    def chunk(g, carry):
        take(g)

        @pl.when(g == 1)
        def _():
            reply(0)
            local(0).start()
            back(0, 0, 1 - xl).start()
            for i in range(2, 2 * STEP):
                back(0, i, i % 2).start()

        @pl.when(g > 1)
        def _():
            reply(g - 1)
            for i in range(2 * STEP):
                back(g - 1, i, i % 2).start()

        forward(g).wait_recv()
        compute(g)
        return carry

    lax.fori_loop(0, CHUNKS, chunk, 0)
    reply(CHUNKS - 1)
    for i in range(2 * STEP):
        back(CHUNKS - 1, i, i % 2).start()

    grads()

    def collect(g, carry):
        pltpu.make_async_copy(ret.at[g], ret.at[g], ret_sem.at[g]).wait()
        for xs in range(2):
            for kq in range(STEP):
                at = (xs * EXP + g * STEP + kq) * RPITCH
                flat[pl.ds(at, RROWS), :] = ret[g, xs * STEP + kq].astype(F32)
        return carry

    lax.fori_loop(0, CHUNKS, collect, 0)

    remote(0, 1 - xl).wait_send()
    back(0, 0, 1 - xl).wait_send()

    def drain(k, carry):
        remote(k, 0).wait_send()
        remote(k, 1).wait_send()
        return carry

    lax.fori_loop(1, EXP, drain, 0)

    def drain_back(i, carry):
        pltpu.make_async_copy(
            rsend.at[0, pl.ds(0, RROWS)], rsend.at[0, pl.ds(0, RROWS)], rs_sem.at[i]
        ).wait()
        return carry

    lax.fori_loop(2, CHUNKS * 2 * STEP, drain_back, 0)

    def drain_pairs(g, carry):
        forward(g).wait_send()
        part(g).wait_send()
        return carry

    lax.fori_loop(0, CHUNKS, drain_pairs, 0)


def finish(
    ids_ref, flat, slots, sg, su, sd, gt_hbm, gr_hbm, gg_hbm, gu_hbm, gd_hbm, got, gtv, grv, sem
):
    pairs = ((sg, gg_hbm), (su, gu_hbm), (sd, gd_hbm), (gtv, gt_hbm), (grv, gr_hbm))
    copies = [pltpu.make_async_copy(v, h, sem.at[i]) for i, (v, h) in enumerate(pairs)]
    for copy in copies[:3]:
        copy.start()
    target = targets(lax.axis_index("expert"))
    tn = (((0,), (0,)), ((), ()))

    def merge(q, carry):
        for h in range(2):
            col = q * 2 + h
            for j in range(CAP):
                near = flat[pl.ds(j * COLS + col, EXP, stride=RPITCH), :]
                far = flat[pl.ds(EXP * RPITCH + j * COLS + col, EXP, stride=RPITCH), :]
                got[j * EXP : (j + 1) * EXP, pl.ds(pl.multiple_of(col * LANES, LANES), LANES)] = (
                    near + far
                ).astype(BF16)
        return carry

    lax.fori_loop(0, COLS // 2, merge, 0)
    line = (
        flat[pl.ds(CAP * COLS, EXP, stride=RPITCH), :]
        + flat[pl.ds(EXP * RPITCH + CAP * COLS, EXP, stride=RPITCH), :]
    )
    spot = jnp.zeros((EXP, TOK), F32)
    for j in range(CAP):
        spot = spot + slots[j * EXP : (j + 1) * EXP, :].astype(F32) * line[:, j : j + 1]
    for q in range(8):
        grv[q : q + 1, :] = jnp.sum(
            jnp.where(ids_ref[q : q + 1, :] == target, spot, 0.0), axis=0, keepdims=True
        ).astype(BF16)

    def place(m, carry):
        at = pl.ds(pl.multiple_of(m * 512, 512), 512)
        gtv[:, at] = lax.dot_general(slots[...], got[:, at], tn, preferred_element_type=F32).astype(BF16)
        pltpu.make_async_copy(gtv.at[:, at], gt_hbm.at[:, at], sem.at[3]).start()
        return carry

    copies[4].start()
    lax.fori_loop(0, FEAT // 512, place, 0)
    for copy in copies:
        copy.wait()


def shards(tokens, out_grad, expert_ids, route_weights, w_gate, w_up, w_down):
    vmem = pl.BlockSpec(memory_space=pltpu.VMEM)
    anywhere = pl.BlockSpec(memory_space=pl.ANY)
    size = 2 * STEP * RROWS
    dma = pltpu.SemaphoreType.DMA
    shapes = ((TOK, FEAT), (8, TOK), (FEAT, HID), (FEAT, HID), (HID, FEAT))
    kept = (((2 * EXP * RPITCH + SPARE, LANES), F32), ((CAP * EXP, TOK), BF16)) + tuple((s, BF16) for s in shapes[2:])
    made = pl.pallas_call(
        body,
        out_shape=tuple(pltpu.VMEM(s, t) for s, t in kept),
        in_specs=[vmem, vmem] + [anywhere] * 5,
        out_specs=(vmem,) * 5,
        scratch_shapes=[
            pltpu.VMEM((FEAT, 2 * HID), BF16),
            pltpu.VMEM((2 * HID, FEAT), BF16),
            pltpu.VMEM((HID, FEAT), BF16),
            pltpu.VMEM((EXP, FROWS, LANES), BF16),
            pltpu.VMEM((CHUNKS, SRC, FROWS, LANES), BF16),
            pltpu.VMEM((ALL, 2 * FEAT), BF16),
            pltpu.VMEM((ALL, 2 * HID), BF16),
            pltpu.VMEM((ALL, HID), BF16),
            pltpu.VMEM((SRC * RPITCH + SPARE, LANES), F32),
            pltpu.VMEM((CHUNKS, size, LANES), BF16),
            pltpu.VMEM((CHUNKS, size, LANES), BF16),
            pltpu.VMEM((CHUNKS, size, LANES), BF16),
            pltpu.VMEM((CHUNKS, size, LANES), BF16),
            pltpu.VMEM((CHUNKS, 2 * STEP, RROWS, LANES), BF16),
            pltpu.VMEM((EXP // 8, CAP * 8, TOK), F32),
            pltpu.VMEM((TOK, FEAT), BF16),
            pltpu.VMEM((TOK, FEAT), BF16),
            dma((2 * EXP,)),
            dma((CHUNKS,)),
            dma((CHUNKS,)),
            dma((CHUNKS,)),
            dma((CHUNKS,)),
            dma((CHUNKS,)),
            dma((2 * EXP,)),
            dma((CHUNKS,)),
            dma((3,)),
            dma((2,)),
        ],
        compiler_params=pltpu.CompilerParams(
            collective_id=0, has_side_effects=True, vmem_limit_bytes=52_000_000
        ),
    )(
        expert_ids.T,
        route_weights.T,
        tokens,
        out_grad,
        w_gate[0],
        w_up[0],
        w_down[0],
    )
    made = [pltpu.with_memory_space_constraint(m, pltpu.VMEM) for m in made]
    grad_tokens, grad_route, grad_g, grad_u, grad_d = pl.pallas_call(
        finish,
        out_shape=tuple(jax.ShapeDtypeStruct(s, BF16) for s in shapes),
        in_specs=[vmem] * 6,
        out_specs=(anywhere,) * 5,
        scratch_shapes=[
            pltpu.VMEM((CAP * EXP, FEAT), BF16),
            pltpu.VMEM((TOK, FEAT), BF16),
            pltpu.VMEM((8, TOK), BF16),
            dma((5,)),
        ],
        compiler_params=pltpu.CompilerParams(vmem_limit_bytes=16_000_000),
    )(expert_ids.T, *made)
    return (grad_tokens, grad_route.T, grad_g[None], grad_u[None], grad_d[None])


def solution(mesh):
    rows_spec = P(("expert", "dp"), None)
    hidden_last = P("expert", None, "dp")
    hidden_mid = P("expert", "dp", None)
    return jax.shard_map(
        shards,
        mesh=mesh,
        in_specs=(rows_spec,) * 4 + (hidden_last, hidden_last, hidden_mid),
        out_specs=(rows_spec, rows_spec, hidden_last, hidden_last, hidden_mid),
        check_vma=False,
    )
```
